512 devices in a mesh: tensor: 8 (over x, core), context: 64 (over z, y).
Axes of the slice: x: 4, y: 8, z: 8, core: 2. Of those that a mesh axis runs over, the one named last changes fastest.
Arguments:
- token_ids: int32 [2, 6144], P(None, 'context'), may hold values from 0 to 151935
- embed_table: bfloat16 [4096, 151936], P('context', 'tensor')
- input_gain: float32 [4096], replicated, may hold values from 0.1 to 1.9
- w_qkv: bfloat16 [4096, 6144], P('context', 'tensor')
- q_gain: float32 [128], replicated, may hold values from 1 to 10
- k_gain: float32 [128], replicated, may hold values from 1 to 10
Outputs:
- attended: bfloat16 [64, 6144, 128], P('context', 'tensor')
The draws below stay inside these ranges and needn't reach their ends.
All inputs are finite; a program needn't handle non-finite values.
Results may differ from the reference program's by a relative error of at most 0.0085.
The reference program's roundings to bfloat16 on the way count: a program that leaves them out, or rounds other values in their place, can miss the bound.
Values may be sent and summed in bfloat16 or wider, within the bound.
A program may use at most 64 MiB of HBM per device.

```python
import math
import jax
import jax.numpy as jnp
import numpy as np
from jax import lax

V = 151936
D = 4096
QH = 32
KVH = 8
HD = 128
SEQS = 2
S = 6144
COLS = 6144


def draw_embed_table(key, part):
    key = jax.random.fold_in(key, 101)
    first, second = jax.random.split(key, 2)
    scales = jnp.exp(jax.random.uniform(first, (D, 1), jnp.float32, 0.0, math.log(10.0)))
    raw = jax.random.normal(second, (D, V), jnp.float32)
    return (raw * scales).astype(jnp.bfloat16)


def draw_w_qkv(key, part):
    key = jax.random.fold_in(key, 202)
    factor = 1.0 / math.sqrt(D)
    raw = jax.random.normal(key, (D, COLS), jnp.float32) * factor
    return raw.astype(jnp.bfloat16)


def draw_gain_common(key, salt):
    key = jax.random.fold_in(key, salt)
    return jnp.exp(jax.random.uniform(key, (HD,), jnp.float32, 0.0, math.log(2.5)))


def draw_q_gain(key, part):
    return draw_gain_common(key, 303)


def draw_k_gain(key, part):
    return draw_gain_common(key, 404)


def touch_ends(entries, stream_key, least, high):
    index_at = [jax.random.randint(jax.random.fold_in(stream_key, axis), (), 0, length) for axis, length in enumerate(entries.shape)]
    widest = entries.shape.index(max(entries.shape))
    beside = index_at[:widest] + [(index_at[widest] + 1) % entries.shape[widest]] + index_at[widest + 1:]
    return entries.at[tuple(index_at)].set(least).at[tuple(beside)].set(high)


def ranked_wide(own_key, shape, amount, skew):
    portions = [min(1 << octave, amount + 1 - (1 << octave)) * (1 << 20) // math.isqrt((1 << octave) ** skew) + 1 for octave in range((amount + 1).bit_length()) if 1 << octave <= amount]
    deviation = 1 + sum(portions) // (1 << 30)
    table = np.cumsum(np.array([max(1, weight // deviation) for weight in portions]))
    pick = jax.random.randint(jax.random.fold_in(own_key, 1), shape, 0, int(table[len(portions) - 1]))
    start = jnp.left_shift(1, jnp.searchsorted(jnp.asarray(table, jnp.int32), pick, side="right").astype(jnp.int32))
    standing = start - 1 + jax.random.randint(jax.random.fold_in(own_key, 4), shape, 0, 1 << 30) % jnp.minimum(start, amount + 1 - start)
    return jax.random.permutation(jax.random.fold_in(own_key, 2), amount)[standing].astype(jnp.int32)


def setup_inputs(seed: int = 0) -> dict:
    seeds = jax.random.split(jax.random.key(seed), 7)
    return {
        "token_ids": touch_ends(ranked_wide(seeds[0], (SEQS, S), V, 2), jax.random.fold_in(seeds[0], 3), 0, V - 1).astype(jnp.int32),
        "embed_table": draw_embed_table(jax.random.fold_in(seeds[6], 71), 0),
        "input_gain": jnp.clip(1.0 + 0.18 * jax.random.normal(seeds[2], (D,), jnp.float32), 0.1, 1.9),
        "w_qkv": draw_w_qkv(jax.random.fold_in(seeds[6], 71), 0),
        "q_gain": draw_q_gain(jax.random.fold_in(seeds[6], 71), 0),
        "k_gain": draw_k_gain(jax.random.fold_in(seeds[6], 71), 0),
    }


ROPE_BASE = 1000000.0
EPSILON = 1e-06
NEGATIVE = -1e+30

def rope_tables(positions, width):
    half_width = width // 2
    exponent = jnp.arange(half_width, dtype=jnp.float32) * (2.0 / width)
    inverse = jnp.exp(-exponent * jnp.log(jnp.float32(ROPE_BASE)))
    angles = positions.astype(jnp.float32)[:, None] * inverse[None, :]
    angles = jnp.concatenate([angles, angles], axis=-1)
    return (jnp.cos(angles), jnp.sin(angles))

def norm_rope(head_vals, head_gain, cos_table, sin_table):
    mean_sq = lax.optimization_barrier(jnp.mean(head_vals * head_vals, axis=-1, keepdims=True))
    scaled = head_vals * lax.rsqrt(mean_sq + EPSILON) * head_gain
    half_width = scaled.shape[-1] // 2
    rotated = jnp.concatenate([-scaled[..., half_width:], scaled[..., :half_width]], axis=-1)
    return scaled * cos_table[:, None, :] + rotated * sin_table[:, None, :]

def reference(token_ids, embed_table, input_gain, w_qkv, q_gain, k_gain):
    embedded = jnp.take(embed_table, token_ids, axis=1)
    hidden = jnp.transpose(embedded, (1, 2, 0)).astype(jnp.float32)
    mean_sq = lax.optimization_barrier(jnp.mean(hidden * hidden, axis=-1, keepdims=True))
    normed = (hidden * lax.rsqrt(mean_sq + EPSILON) * input_gain).astype(jnp.bfloat16)
    joined = jnp.dot(normed.reshape(SEQS * S, D), w_qkv, preferred_element_type=jnp.float32)
    joined = joined.astype(jnp.bfloat16).reshape(SEQS, S, COLS)
    wide = joined.astype(jnp.float32)
    cos_table, sin_table = rope_tables(jnp.arange(S, dtype=jnp.int32), HD)
    queries = norm_rope(wide[..., :QH * HD].reshape(SEQS, S, QH, HD), q_gain, cos_table, sin_table).astype(jnp.bfloat16)
    key_heads = norm_rope(wide[..., QH * HD:(QH + KVH) * HD].reshape(SEQS, S, KVH, HD), k_gain, cos_table, sin_table).astype(jnp.bfloat16)
    values = joined[..., (QH + KVH) * HD:].reshape(SEQS, S, KVH, HD)
    group_size = QH // KVH
    queries = jnp.transpose(queries, (0, 2, 1, 3)).reshape(SEQS * QH, S, HD)
    key_heads = jnp.repeat(jnp.transpose(key_heads, (0, 2, 1, 3)), group_size, axis=1).reshape(SEQS * QH, S, HD)
    values = jnp.repeat(jnp.transpose(values, (0, 2, 1, 3)), group_size, axis=1).reshape(SEQS * QH, S, HD)
    causal = jnp.arange(S)[:, None] >= jnp.arange(S)[None, :]
    score_scale = HD ** (-0.5)

    def one_unit(operands):
        query_rows, key_rows, value_rows = operands
        scores = jnp.dot(query_rows.astype(jnp.float32), key_rows.astype(jnp.float32).T) * score_scale
        scores = jnp.where(causal, scores, NEGATIVE)
        row_max = lax.optimization_barrier(jnp.max(scores, axis=-1, keepdims=True))
        raised = jnp.where(causal, jnp.exp(scores - row_max), 0.0)
        total = lax.optimization_barrier(jnp.sum(raised, axis=-1, keepdims=True))
        weights = raised.astype(jnp.bfloat16)
        summed = jnp.dot(weights.astype(jnp.float32), value_rows.astype(jnp.float32))
        return (summed / total).astype(jnp.bfloat16)
    return lax.map(one_unit, (queries, key_heads, values))
```

```python
import functools

import jax
import jax.numpy as jnp
from jax import lax
from jax.experimental import pallas as pl
from jax.experimental.pallas import tpu as pltpu
from jax.sharding import PartitionSpec as P

QH = 32
KVH = 8
HD = 128
ROPE_BASE = 1000000.0
EPSILON = 1e-06
NEGATIVE = -1e30
MESH = pl.DeviceIdType.MESH
VMEM_LIMIT = 60 * 1024 * 1024


def rope_tables(positions, width):
    half_width = width // 2
    exponent = jnp.arange(half_width, dtype=jnp.float32) * (2.0 / width)
    inverse = jnp.exp(-exponent * jnp.log(jnp.float32(ROPE_BASE)))
    angles = positions.astype(jnp.float32)[:, None] * inverse[None, :]
    angles = jnp.concatenate([angles, angles], axis=-1)
    return (jnp.cos(angles), jnp.sin(angles))


def remote(src, dst, send_sem, recv_sem, t, c):
    return pltpu.make_async_remote_copy(
        src_ref=src, dst_ref=dst, send_sem=send_sem, recv_sem=recv_sem,
        device_id=(t, c), device_id_type=MESH)


def greet(barrier, t, c, me_t, me_c):
    own = jnp.logical_and(t == me_t, c == me_c)

    @pl.when(jnp.logical_not(own))
    def _():
        pl.semaphore_signal(barrier, inc=1, device_id=(t, c), device_id_type=MESH)

    return own.astype(jnp.int32)


K0 = 8
V0 = 72
W_CHUNKS = 8


def attention_kernel(x_ref, w_hbm, cos_ref, sin_ref, qg_ref, kg_ref, o_ref,
                     w_buf, acc_ref, heads, blocks, w_sem,
                     s1_send, s1_recv, s2_send, s2_recv, s3_send, s3_recv,
                     s4_send, s4_recv):
    t = lax.axis_index("tensor")
    c = lax.axis_index("context")
    x, k = t // 2, t % 2
    chunk = w_buf.shape[1]
    w_copies = [
        pltpu.make_async_copy(w_hbm.at[pl.ds(i * chunk, chunk)], w_buf.at[i], w_sem.at[i])
        for i in range(W_CHUNKS)
    ]
    for w_copy in w_copies:
        w_copy.start()

    head_u = c % QH
    group_u = head_u // 4
    y4 = head_u % 4
    barrier = pltpu.get_barrier_semaphore()
    kept = jnp.int32(0)
    for i in range(8):
        kept += greet(barrier, head_u // 6, 8 * t + i, t, c)
    for i in range(2):
        kept += greet(barrier, (QH + group_u) // 6, 8 * t + 2 * y4 + i, t, c)
        kept += greet(barrier, (QH + KVH + group_u) // 6, 8 * t + 2 * y4 + i, t, c)
    for d in range(1, 4):
        pl.semaphore_signal(barrier, inc=1, device_id=(t, c - y4 + (y4 + d) % 4), device_id_type=MESH)
    for d in range(1, 8):
        pl.semaphore_signal(barrier, inc=1, device_id=((t + d) % 8, c), device_id_type=MESH)

    for i in range(W_CHUNKS):
        w_copies[i].wait()
        part = jnp.dot(x_ref[:, i * chunk:(i + 1) * chunk], w_buf[i],
                       preferred_element_type=jnp.float32)
        if i == 0:
            acc_ref[...] = part
        else:
            acc_ref[...] += part

    cos_t, sin_t = cos_ref[...], sin_ref[...]
    for j in range(6):
        head = 6 * t + j
        gain = jnp.where(head < QH, qg_ref[...], kg_ref[...])
        for s in range(2):
            raw = acc_ref[96 * s:96 * s + 96, 128 * j:128 * j + 128].astype(jnp.bfloat16)
            wide = raw.astype(jnp.float32)
            mean_sq = jnp.mean(wide * wide, axis=-1, keepdims=True)
            scaled = wide * lax.rsqrt(mean_sq + EPSILON) * gain
            turned = scaled * cos_t + pltpu.roll(scaled, 64, 1) * sin_t
            heads[6 * s + j] = jnp.where(head < QH + KVH, turned, wide).astype(jnp.bfloat16)

    pl.semaphore_wait(barrier, 22 - kept)

    def stage1(b, start):
        s, j = b // 6, b % 6
        head = 6 * t + j
        is_q = head < QH
        i = jnp.maximum(head - QH, 0)
        kind, group = i // KVH, i % KVH
        to_c = s * QH + jnp.where(is_q, head, 4 * group + (c % 8) // 2)
        to_t = c // 8
        slot = jnp.where(is_q, c % 8, K0 + 64 * kind + c)
        sem = jnp.where(is_q, c % 8, 8 + 2 * kind + c % 2)
        own = jnp.logical_and(to_t == t, to_c == c)
        far = remote(heads.at[b], blocks.at[slot], s1_send.at[b], s1_recv.at[sem], to_t, to_c)

        @pl.when(own)
        def _():
            if start:
                pltpu.make_async_copy(heads.at[b], blocks.at[slot], s1_recv.at[sem]).start()

        @pl.when(jnp.logical_not(own))
        def _():
            if start:
                far.start()
            else:
                far.wait_send()

    def land(dst, sem):
        pltpu.make_async_copy(dst, dst, sem).wait()

    for b in range(12):
        stage1(b, True)
    base = 8 * t + 2 * y4
    for i in range(2):
        land(blocks.at[K0 + base + i], s1_recv.at[8 + i])
        land(blocks.at[V0 + base + i], s1_recv.at[10 + i])

    def stage2(kind, d):
        first = (K0, V0)[kind] + base
        peer = (y4 + d) % 4
        return remote(blocks.at[pl.ds(first, 2)], blocks.at[pl.ds(first, 2)],
                      s2_send.at[kind, d], s2_recv.at[kind, y4], t, c - y4 + peer)

    for kind in range(2):
        for d in range(1, 4):
            stage2(kind, d).start()
    for kind in range(2):
        for d in range(1, 4):
            peer = (y4 + d) % 4
            land(blocks.at[pl.ds((K0, V0)[kind] + 8 * t + 2 * peer, 2)], s2_recv.at[kind, peer])

    def slab(kind, tt):
        return blocks.at[pl.ds((K0, V0)[kind] + 8 * tt, 8)]

    def along_x(kind, of, to, n):
        return remote(slab(kind, 2 * of + k), slab(kind, 2 * of + k),
                      s3_send.at[n], s3_recv.at[kind, of], 2 * to + k, c)

    def arrived_x(kind, of):
        land(slab(kind, 2 * of + k), s3_recv.at[kind, of])

    def across(kind, of):
        return remote(slab(kind, 2 * of + k), slab(kind, 2 * of + k),
                      s4_send.at[kind, of], s4_recv.at[kind, of], 2 * x + 1 - k, c)

    def across_here(kind, of):
        last = jnp.where(k == 0, x, x - 1)
        return of <= last

    def hand_on(kind, of):
        @pl.when(across_here(kind, of))
        def _():
            across(kind, of).start()

    own_list = {
        0: [(0, 0, 1), (1, 0, 1), (0, 0, 3), (1, 0, 3)],
        1: [(1, 1, 0), (0, 1, 2), (1, 1, 2)],
        2: [(0, 2, 3), (1, 2, 3)],
        3: [],
    }
    relay_list = {0: [(1, 1, 3)], 1: [(0, 0, 2)], 2: [(0, 1, 3)], 3: [(1, 0, 2)]}
    get_list = {
        0: [],
        1: [(0, 0), (1, 0)],
        2: [(0, 1), (1, 1), (0, 0), (1, 0)],
        3: [(1, 0), (0, 0), (0, 2), (1, 2), (0, 1), (1, 1)],
    }
    for xx in range(4):
        @pl.when(x == xx)
        def _(xx=xx):
            for n, (kind, of, to) in enumerate(own_list[xx]):
                along_x(kind, of, to, n).start()
            for kind in range(2):
                @pl.when(k == 0)
                def _():
                    across(kind, xx).start()
            done = set()
            for n, (kind, of, to) in enumerate(relay_list[xx]):
                arrived_x(kind, of)
                done.add((kind, of))
                along_x(kind, of, to, len(own_list[xx]) + n).start()
                if of < xx:
                    across(kind, of).start()
            for kind, of in get_list[xx]:
                if (kind, of) not in done:
                    arrived_x(kind, of)
                    across(kind, of).start()

    for of in range(4):
        for kind in range(2):
            @pl.when(jnp.where(k == 1, of <= x, of < x))
            def _():
                land(slab(kind, 2 * of + 1 - k), s4_recv.at[kind, of])

    for i in range(8):
        land(blocks.at[i], s1_recv.at[i])

    score_scale = HD ** (-0.5)
    rows = 256

    def update(state, q, keys, vals, mask):
        old_max, old_total, old_acc = state
        scores = lax.dot_general(q, keys, (((1,), (1,)), ((), ())),
                                 preferred_element_type=jnp.float32) * score_scale
        if mask is not None:
            scores = jnp.where(mask, scores, NEGATIVE)
        new_max = jnp.maximum(old_max, jnp.max(scores, axis=-1, keepdims=True))
        weights = jnp.exp(scores - new_max)
        shrink = jnp.exp(old_max - new_max)
        new_total = old_total * shrink + jnp.sum(weights, axis=-1, keepdims=True)
        new_acc = old_acc * shrink + jnp.dot(
            weights.astype(jnp.bfloat16), vals, preferred_element_type=jnp.float32)
        return new_max, new_total, new_acc

    for i in range(3):
        q = blocks[0:8].reshape(768, HD)[rows * i:rows * (i + 1)]
        width = rows * (i + 1)
        keys = blocks[pl.ds(K0 + 8 * t, 8)].reshape(768, HD)[:width]
        vals = blocks[pl.ds(V0 + 8 * t, 8)].reshape(768, HD)[:width]
        mask = (lax.broadcasted_iota(jnp.int32, (rows, width), 1)
                <= lax.broadcasted_iota(jnp.int32, (rows, width), 0) + rows * i)
        state = (jnp.full((rows, 1), NEGATIVE, jnp.float32),
                 jnp.zeros((rows, 1), jnp.float32),
                 jnp.zeros((rows, HD), jnp.float32))
        state = update(state, q, keys, vals, mask)

        def step(tt, state, q=q):
            keys = blocks[pl.ds(K0 + 8 * tt, 8)].reshape(768, HD)
            vals = blocks[pl.ds(V0 + 8 * tt, 8)].reshape(768, HD)
            return update(state, q, keys, vals, None)

        _, total, acc = lax.fori_loop(0, t, step, state)
        o_ref[0, rows * i:rows * (i + 1), :] = (acc / total).astype(jnp.bfloat16)

    for b in range(12):
        stage1(b, False)
    for kind in range(2):
        for d in range(1, 4):
            stage2(kind, d).wait_send()
    for xx in range(4):
        @pl.when(x == xx)
        def _(xx=xx):
            sends = own_list[xx] + relay_list[xx]
            for n, (kind, of, to) in enumerate(sends):
                along_x(kind, of, to, n).wait_send()
    for of in range(4):
        for kind in range(2):
            @pl.when(across_here(kind, of))
            def _():
                across(kind, of).wait_send()


def attention(normed, w_all, cos_t, sin_t, q_gain, k_gain):
    vmem = pl.BlockSpec(memory_space=pltpu.VMEM)
    dma = pltpu.SemaphoreType.DMA
    return pl.pallas_call(
        attention_kernel,
        out_shape=jax.ShapeDtypeStruct((1, 768, HD), jnp.bfloat16),
        in_specs=[vmem, pl.BlockSpec(memory_space=pl.ANY), vmem, vmem, vmem, vmem],
        out_specs=vmem,
        scratch_shapes=[
            pltpu.VMEM((W_CHUNKS, 4096 // W_CHUNKS, 768), jnp.bfloat16),
            pltpu.VMEM((192, 768), jnp.float32),
            pltpu.VMEM((12, 96, HD), jnp.bfloat16),
            pltpu.VMEM((136, 96, HD), jnp.bfloat16),
            dma((W_CHUNKS,)),
            dma((12,)), dma((12,)),
            dma((2, 4)), dma((2, 4)),
            dma((6,)), dma((2, 4)),
            dma((2, 4)), dma((2, 4)),
        ],
        compiler_params=pltpu.CompilerParams(
            collective_id=1, has_side_effects=True, vmem_limit_bytes=VMEM_LIMIT),
        name="project_exchange_attend",
    )(normed, w_all, cos_t, sin_t, q_gain, k_gain)


def feature_norm(embedded, input_gain):
    hidden = embedded.astype(jnp.float32)
    mean_sq = jnp.mean(hidden * hidden, axis=0, keepdims=True)
    return (hidden * lax.rsqrt(mean_sq + EPSILON) * input_gain[:, None, None]).astype(jnp.bfloat16)


def shards(token_ids, embed_table, input_gain, w_qkv, q_gain, k_gain):
    tensor_rank = lax.axis_index("tensor")
    context_rank = lax.axis_index("context")
    seq_count, local_len = token_ids.shape
    width_part, vocab_part = embed_table.shape
    w_all = lax.all_gather(w_qkv, "context", axis=0, tiled=True)
    all_ids = lax.all_gather(token_ids, "context", axis=1, tiled=True)
    local_ids = all_ids - tensor_rank * vocab_part
    inside = (local_ids >= 0) & (local_ids < vocab_part)
    picked = jnp.take(embed_table, jnp.clip(local_ids, 0, vocab_part - 1), axis=1)
    partial_rows = jnp.where(inside[None], picked.astype(jnp.float32), 0.0)
    summed = lax.psum(partial_rows.astype(jnp.bfloat16), "tensor")
    embedded = lax.all_to_all(summed, "context", split_axis=2, concat_axis=0, tiled=True)
    normed = feature_norm(embedded, input_gain)
    normed = jnp.transpose(normed, (1, 2, 0)).reshape(seq_count * local_len, -1)
    positions = context_rank * local_len + jnp.arange(local_len, dtype=jnp.int32)
    cos_t, sin_t = rope_tables(positions, HD)
    sin_t = jnp.concatenate([-sin_t[:, :64], sin_t[:, 64:]], axis=-1)
    return attention(normed, w_all, cos_t, sin_t, q_gain[None], k_gain[None])


def solution(mesh):
    return jax.shard_map(
        shards,
        mesh=mesh,
        in_specs=(P(None, "context"), P("context", "tensor"), P(), P("context", "tensor"), P(), P()),
        out_specs=P("context", "tensor", None),
        check_vma=False,
    )
```

```python
import functools

import jax
import jax.numpy as jnp
from jax import lax
from jax.experimental import pallas as pl
from jax.experimental.pallas import tpu as pltpu
from jax.sharding import PartitionSpec as P

QH = 32
KVH = 8
HD = 128
ROPE_BASE = 1000000.0
EPSILON = 1e-06
NEGATIVE = -1e30
MESH = pl.DeviceIdType.MESH
VMEM_LIMIT = 60 * 1024 * 1024


def rope_tables(positions, width):
    half_width = width // 2
    exponent = jnp.arange(half_width, dtype=jnp.float32) * (2.0 / width)
    inverse = jnp.exp(-exponent * jnp.log(jnp.float32(ROPE_BASE)))
    angles = positions.astype(jnp.float32)[:, None] * inverse[None, :]
    angles = jnp.concatenate([angles, angles], axis=-1)
    return (jnp.cos(angles), jnp.sin(angles))


def remote(src, dst, send_sem, recv_sem, t, c):
    return pltpu.make_async_remote_copy(
        src_ref=src, dst_ref=dst, send_sem=send_sem, recv_sem=recv_sem,
        device_id=(t, c), device_id_type=MESH)


def greet(barrier, t, c, me_t, me_c):
    own = jnp.logical_and(t == me_t, c == me_c)

    @pl.when(jnp.logical_not(own))
    def _():
        pl.semaphore_signal(barrier, inc=1, device_id=(t, c), device_id_type=MESH)

    return own.astype(jnp.int32)


K0 = 8
V0 = 72
W_CHUNKS = 8


def attention_kernel(x_ref, w_hbm, cos_ref, sin_ref, qg_ref, kg_ref, o_ref,
                     w_buf, acc_ref, heads, blocks, w_sem,
                     s1_send, s1_recv, s2_send, s2_recv, s3_send, s3_recv,
                     s4_send, s4_recv):
    t = lax.axis_index("tensor")
    c = lax.axis_index("context")
    x, k = t // 2, t % 2
    chunk = w_buf.shape[1]
    w_copies = [
        pltpu.make_async_copy(w_hbm.at[pl.ds(i * chunk, chunk)], w_buf.at[i], w_sem.at[i])
        for i in range(W_CHUNKS)
    ]
    for w_copy in w_copies:
        w_copy.start()

    head_u = c % QH
    group_u = head_u // 4
    y4 = head_u % 4
    barrier = pltpu.get_barrier_semaphore()
    kept = jnp.int32(0)
    for i in range(8):
        kept += greet(barrier, head_u // 6, 8 * t + i, t, c)
    for i in range(2):
        kept += greet(barrier, (QH + group_u) // 6, 8 * t + 2 * y4 + i, t, c)
        kept += greet(barrier, (QH + KVH + group_u) // 6, 8 * t + 2 * y4 + i, t, c)
    for d in range(1, 4):
        pl.semaphore_signal(barrier, inc=1, device_id=(t, c - y4 + (y4 + d) % 4), device_id_type=MESH)
    for d in range(1, 8):
        pl.semaphore_signal(barrier, inc=1, device_id=((t + d) % 8, c), device_id_type=MESH)

    for i in range(W_CHUNKS):
        w_copies[i].wait()
        at = i % 4 * chunk
        lhs = x_ref[:, i // 4, :, at:at + chunk].reshape(192, chunk)
        part = jnp.dot(lhs, w_buf[i], preferred_element_type=jnp.float32)
        if i == 0:
            acc_ref[...] = part
        else:
            acc_ref[...] += part

    cos_t, sin_t = cos_ref[...], sin_ref[...]
    for j in range(6):
        head = 6 * t + j
        gain = jnp.where(head < QH, qg_ref[...], kg_ref[...])
        for s in range(2):
            raw = acc_ref[96 * s:96 * s + 96, 128 * j:128 * j + 128].astype(jnp.bfloat16)
            wide = raw.astype(jnp.float32)
            mean_sq = jnp.mean(wide * wide, axis=-1, keepdims=True)
            scaled = wide * lax.rsqrt(mean_sq + EPSILON) * gain
            turned = scaled * cos_t + pltpu.roll(scaled, 64, 1) * sin_t
            heads[6 * s + j] = jnp.where(head < QH + KVH, turned, wide).astype(jnp.bfloat16)

    pl.semaphore_wait(barrier, 22 - kept)

    def stage1(b, start):
        s, j = b // 6, b % 6
        head = 6 * t + j
        is_q = head < QH
        i = jnp.maximum(head - QH, 0)
        kind, group = i // KVH, i % KVH
        to_c = s * QH + jnp.where(is_q, head, 4 * group + (c % 8) // 2)
        to_t = c // 8
        slot = jnp.where(is_q, c % 8, K0 + 64 * kind + c)
        sem = jnp.where(is_q, c % 8, 8 + 2 * kind + c % 2)
        own = jnp.logical_and(to_t == t, to_c == c)
        far = remote(heads.at[b], blocks.at[slot], s1_send.at[b], s1_recv.at[sem], to_t, to_c)

        @pl.when(own)
        def _():
            if start:
                pltpu.make_async_copy(heads.at[b], blocks.at[slot], s1_recv.at[sem]).start()

        @pl.when(jnp.logical_not(own))
        def _():
            if start:
                far.start()
            else:
                far.wait_send()

    def land(dst, sem):
        pltpu.make_async_copy(dst, dst, sem).wait()

    for b in range(12):
        stage1(b, True)
    base = 8 * t + 2 * y4
    for i in range(2):
        land(blocks.at[K0 + base + i], s1_recv.at[8 + i])
        land(blocks.at[V0 + base + i], s1_recv.at[10 + i])

    def stage2(kind, d):
        first = (K0, V0)[kind] + base
        peer = (y4 + d) % 4
        return remote(blocks.at[pl.ds(first, 2)], blocks.at[pl.ds(first, 2)],
                      s2_send.at[kind, d], s2_recv.at[kind, y4], t, c - y4 + peer)

    for kind in range(2):
        for d in range(1, 4):
            stage2(kind, d).start()
    for kind in range(2):
        for d in range(1, 4):
            peer = (y4 + d) % 4
            land(blocks.at[pl.ds((K0, V0)[kind] + 8 * t + 2 * peer, 2)], s2_recv.at[kind, peer])

    def slab(kind, tt):
        return blocks.at[pl.ds((K0, V0)[kind] + 8 * tt, 8)]

    def along_x(kind, of, to, n):
        return remote(slab(kind, 2 * of + k), slab(kind, 2 * of + k),
                      s3_send.at[n], s3_recv.at[kind, of], 2 * to + k, c)

    def arrived_x(kind, of):
        land(slab(kind, 2 * of + k), s3_recv.at[kind, of])

    def across(kind, of):
        return remote(slab(kind, 2 * of + k), slab(kind, 2 * of + k),
                      s4_send.at[kind, of], s4_recv.at[kind, of], 2 * x + 1 - k, c)

    def across_here(kind, of):
        last = jnp.where(k == 0, x, x - 1)
        return of <= last

    def hand_on(kind, of):
        @pl.when(across_here(kind, of))
        def _():
            across(kind, of).start()

    own_list = {
        0: [(0, 0, 1), (1, 0, 1), (0, 0, 3), (1, 0, 3)],
        1: [(1, 1, 0), (0, 1, 2), (1, 1, 2)],
        2: [(0, 2, 3), (1, 2, 3)],
        3: [],
    }
    relay_list = {0: [(1, 1, 3)], 1: [(0, 0, 2)], 2: [(0, 1, 3)], 3: [(1, 0, 2)]}
    get_list = {
        0: [],
        1: [(0, 0), (1, 0)],
        2: [(0, 1), (1, 1), (0, 0), (1, 0)],
        3: [(1, 0), (0, 0), (0, 2), (1, 2), (0, 1), (1, 1)],
    }
    for xx in range(4):
        @pl.when(x == xx)
        def _(xx=xx):
            for n, (kind, of, to) in enumerate(own_list[xx]):
                along_x(kind, of, to, n).start()
            for kind in range(2):
                @pl.when(k == 0)
                def _():
                    across(kind, xx).start()
            done = set()
            for n, (kind, of, to) in enumerate(relay_list[xx]):
                arrived_x(kind, of)
                done.add((kind, of))
                along_x(kind, of, to, len(own_list[xx]) + n).start()
                if of < xx:
                    across(kind, of).start()
            for kind, of in get_list[xx]:
                if (kind, of) not in done:
                    arrived_x(kind, of)
                    across(kind, of).start()

    for of in range(4):
        for kind in range(2):
            @pl.when(jnp.where(k == 1, of <= x, of < x))
            def _():
                land(slab(kind, 2 * of + 1 - k), s4_recv.at[kind, of])

    for i in range(8):
        land(blocks.at[i], s1_recv.at[i])

    score_scale = HD ** (-0.5)
    rows = 256

    def update(state, q, keys, vals, mask):
        old_max, old_total, old_acc = state
        scores = lax.dot_general(q, keys, (((1,), (1,)), ((), ())),
                                 preferred_element_type=jnp.float32) * score_scale
        if mask is not None:
            scores = jnp.where(mask, scores, NEGATIVE)
        new_max = jnp.maximum(old_max, jnp.max(scores, axis=-1, keepdims=True))
        weights = jnp.exp(scores - new_max)
        shrink = jnp.exp(old_max - new_max)
        new_total = old_total * shrink + jnp.sum(weights, axis=-1, keepdims=True)
        new_acc = old_acc * shrink + jnp.dot(
            weights.astype(jnp.bfloat16), vals, preferred_element_type=jnp.float32)
        return new_max, new_total, new_acc

    for i in range(3):
        q = blocks[0:8].reshape(768, HD)[rows * i:rows * (i + 1)]
        width = rows * (i + 1)
        keys = blocks[pl.ds(K0 + 8 * t, 8)].reshape(768, HD)[:width]
        vals = blocks[pl.ds(V0 + 8 * t, 8)].reshape(768, HD)[:width]
        mask = (lax.broadcasted_iota(jnp.int32, (rows, width), 1)
                <= lax.broadcasted_iota(jnp.int32, (rows, width), 0) + rows * i)
        state = (jnp.full((rows, 1), NEGATIVE, jnp.float32),
                 jnp.zeros((rows, 1), jnp.float32),
                 jnp.zeros((rows, HD), jnp.float32))
        state = update(state, q, keys, vals, mask)

        def step(tt, state, q=q):
            keys = blocks[pl.ds(K0 + 8 * tt, 8)].reshape(768, HD)
            vals = blocks[pl.ds(V0 + 8 * tt, 8)].reshape(768, HD)
            return update(state, q, keys, vals, None)

        _, total, acc = lax.fori_loop(0, t, step, state)
        o_ref[0, rows * i:rows * (i + 1), :] = (acc / total).astype(jnp.bfloat16)

    for b in range(12):
        stage1(b, False)
    for kind in range(2):
        for d in range(1, 4):
            stage2(kind, d).wait_send()
    for xx in range(4):
        @pl.when(x == xx)
        def _(xx=xx):
            sends = own_list[xx] + relay_list[xx]
            for n, (kind, of, to) in enumerate(sends):
                along_x(kind, of, to, n).wait_send()
    for of in range(4):
        for kind in range(2):
            @pl.when(across_here(kind, of))
            def _():
                across(kind, of).wait_send()


def attention(normed, w_all, cos_t, sin_t, q_gain, k_gain):
    vmem = pl.BlockSpec(memory_space=pltpu.VMEM)
    dma = pltpu.SemaphoreType.DMA
    return pl.pallas_call(
        attention_kernel,
        out_shape=jax.ShapeDtypeStruct((1, 768, HD), jnp.bfloat16),
        in_specs=[vmem, pl.BlockSpec(memory_space=pl.ANY), vmem, vmem, vmem, vmem],
        out_specs=vmem,
        scratch_shapes=[
            pltpu.VMEM((W_CHUNKS, 4096 // W_CHUNKS, 768), jnp.bfloat16),
            pltpu.VMEM((192, 768), jnp.float32),
            pltpu.VMEM((12, 96, HD), jnp.bfloat16),
            pltpu.VMEM((136, 96, HD), jnp.bfloat16),
            dma((W_CHUNKS,)),
            dma((12,)), dma((12,)),
            dma((2, 4)), dma((2, 4)),
            dma((6,)), dma((2, 4)),
            dma((2, 4)), dma((2, 4)),
        ],
        compiler_params=pltpu.CompilerParams(
            collective_id=1, has_side_effects=True, vmem_limit_bytes=VMEM_LIMIT),
        name="project_exchange_attend",
    )(normed, w_all, cos_t, sin_t, q_gain, k_gain)


VOCAB_PART = 18992
ZERO_ROW = VOCAB_PART


def embed_kernel(ids_ref, table_ref, gain_ref, out_ref,
                 rows_ref, ids_v, ids_t, ids_s, low, high,
                 for_other, own, from_other, from_x, summed, pieces, wide_ref, normed,
                 ids_send, ids_recv, idx_sem, rs4_send, rs4_recv, rsx_send, rsx_recv,
                 a2a_send, a2a_recv, agx_send, agx_recv, agr_send, agr_recv, agp_send, agp_recv):
    t = lax.axis_index("tensor")
    c = lax.axis_index("context")
    x, k = t // 2, t % 2
    other = 2 * x + 1 - k
    barrier = pltpu.get_barrier_semaphore()

    @pl.loop(1, 64)
    def _(i):
        pl.semaphore_signal(barrier, inc=1, device_id=(t, (c + i) % 64), device_id_type=MESH)

    for d in range(1, 8):
        pl.semaphore_signal(barrier, inc=1, device_id=((t + d) % 8, c), device_id_type=MESH)

    def transpose(block):
        wide = block.astype(jnp.float32)
        return jnp.concatenate([wide, wide], axis=0).T

    full = VOCAB_PART // 128

    def turn(first, last):
        @pl.loop(first, last, unroll=2)
        def _(b):
            at = pl.multiple_of(b * 128, 128)
            rows_ref[pl.ds(at, 128), :] = transpose(table_ref[:, pl.ds(at, 128)])

    turn(0, full // 2)
    pl.semaphore_wait(barrier, 70)

    def send_ids(i):
        return remote(ids_ref, ids_v.at[c], ids_send.at[i], ids_recv.at[c], t, (c + i) % 64)

    @pl.loop(1, 64)
    def _(i):
        send_ids(i).start()

    ids_v[c] = ids_ref[...]
    turn(full // 2, full)
    rest = VOCAB_PART - full * 128
    tail = jnp.concatenate(
        [table_ref[:, full * 128:].astype(jnp.float32), jnp.zeros((64, 128 - rest), jnp.float32)], axis=1)
    rows_ref[full * 128:, :] = transpose(tail)

    def land(dst, sem):
        pltpu.make_async_copy(dst, dst, sem).wait()

    @pl.loop(1, 64)
    def _(i):
        src = (c + i) % 64
        land(ids_v.at[src], ids_recv.at[src])

    local = ids_v[...] - t * VOCAB_PART
    ids_t[...] = jnp.where(jnp.logical_and(local >= 0, local < VOCAB_PART), local, ZERO_ROW)
    to_smem = pltpu.make_async_copy(ids_t, ids_s, idx_sem)
    to_smem.start()
    to_smem.wait()

    first_half = lax.broadcasted_iota(jnp.int32, (16, 128), 1) < 64

    def look_up(tp, dst, n):
        s = tp // 4
        start = 24 * (tp % 4)

        @pl.loop(0, 32)
        def _(half):
            for m in range(2):
                cc = 2 * half + m
                for i in range(12):
                    low[m, i:i + 1, :] = rows_ref[pl.ds(ids_s[cc, s, start + i], 1), :]
                for i in range(12):
                    high[m, i:i + 1, :] = rows_ref[pl.ds(ids_s[cc, s, start + 12 + i], 1), :]
            for m in range(2):
                dst[n, 2 * half + m] = jnp.where(first_half, low[m], high[m]).astype(jnp.bfloat16)

    low[...] = jnp.zeros_like(low)
    high[...] = jnp.zeros_like(high)

    def to_other(n):
        return remote(for_other.at[n], from_other.at[n], rs4_send.at[n], rs4_recv.at[n], other, c)

    def to_chip(n, xx):
        return remote(own.at[n], from_x.at[n], rsx_send.at[n], rsx_recv.at[n], 2 * xx + k, c)

    for n, d in enumerate((2, 1, 3, 0)):
        xx = (x + d) % 4
        look_up(2 * xx + 1 - k, for_other, n)
        to_other(n).start()
        look_up(2 * xx + k, own, n)
        land(from_other.at[n], rs4_recv.at[n])
        own[n] = own[n] + from_other[n]
        if d:
            to_chip(n, xx).start()

    for n in range(3):
        land(from_x.at[n], rsx_recv.at[n])
    summed[...] = (own[3] + from_x[0]) + (from_x[1] + from_x[2])

    def send_rows(i):
        peer = (c + i) % 64
        return remote(summed.at[peer], pieces.at[c], a2a_send.at[i], a2a_recv.at[c], t, peer)

    @pl.loop(1, 64)
    def _(i):
        send_rows(i).start()

    pieces[c] = summed[c]

    @pl.loop(1, 64)
    def _(i):
        src = (c + i) % 64
        land(pieces.at[src], a2a_recv.at[src])

    def add_squares(i, acc):
        piece = pieces[i].astype(jnp.float32)
        return acc + piece * piece

    squares = lax.fori_loop(0, 64, add_squares, jnp.zeros((16, 128), jnp.float32))
    sum_low = jnp.sum(jnp.where(first_half, squares, 0.0), axis=-1, keepdims=True)
    sum_high = jnp.sum(jnp.where(first_half, 0.0, squares), axis=-1, keepdims=True)
    scale_low = lax.rsqrt(sum_low / 4096 + EPSILON)
    scale_high = lax.rsqrt(sum_high / 4096 + EPSILON)
    for p in range(32):
        even = pieces[2 * p].astype(jnp.float32)
        odd = pieces[2 * p + 1].astype(jnp.float32)
        gain = gain_ref[:, 128 * p:128 * p + 128]
        low_rows = jnp.where(first_half, even, pltpu.roll(odd, 64, 1)) * scale_low * gain
        high_rows = jnp.where(first_half, pltpu.roll(even, 64, 1), odd) * scale_high * gain
        wide_ref[0:12, 128 * p:128 * p + 128] = low_rows[:12]
        wide_ref[12:24, 128 * p:128 * p + 128] = high_rows[:12]
    for h in range(2):
        part = wide_ref[:, 2048 * h:2048 * h + 2048].astype(jnp.bfloat16)
        normed[h] = part
        out_ref[t, h] = part

    right, left = 2 * ((x + 1) % 4) + k, 2 * ((x + 3) % 4) + k
    across = 2 * ((x + 2) % 4) + k
    to_right = remote(normed, out_ref.at[t], agx_send.at[0], agx_recv.at[0], right, c)
    to_left = remote(normed, out_ref.at[t], agx_send.at[1], agx_recv.at[1], left, c)
    to_right.start()
    to_left.start()

    def hand_over(src, tt, n):
        return remote(src, out_ref.at[tt], agp_send.at[n], agp_recv.at[n], other, c)

    hand_own = hand_over(normed, t, 0)
    hand_own.start()
    land(out_ref.at[left], agx_recv.at[0])
    on_right = remote(out_ref.at[left, 0], out_ref.at[left, 0], agr_send.at[0], agr_recv.at[0], right, c)
    on_right.start()
    hand_left = hand_over(out_ref.at[left], left, 1)
    hand_left.start()
    land(out_ref.at[right], agx_recv.at[1])
    on_left = remote(out_ref.at[right, 1], out_ref.at[right, 1], agr_send.at[1], agr_recv.at[1], left, c)
    on_left.start()
    hand_right = hand_over(out_ref.at[right], right, 2)
    hand_right.start()
    land(out_ref.at[across, 0], agr_recv.at[0])
    land(out_ref.at[across, 1], agr_recv.at[1])
    hand_across = hand_over(out_ref.at[across], across, 3)
    hand_across.start()

    flip = 1 - 2 * k
    land(out_ref.at[t + flip], agp_recv.at[0])
    land(out_ref.at[left + flip], agp_recv.at[1])
    land(out_ref.at[right + flip], agp_recv.at[2])
    land(out_ref.at[across + flip], agp_recv.at[3])

    @pl.loop(1, 64)
    def _(i):
        send_ids(i).wait_send()
        send_rows(i).wait_send()

    for n, d in enumerate((2, 1, 3, 0)):
        to_other(n).wait_send()
        if d:
            to_chip(n, (x + d) % 4).wait_send()
    for copy in (to_right, to_left, on_right, on_left, hand_own, hand_left, hand_right, hand_across):
        copy.wait_send()


def embed(ids, table, gain):
    vmem = pl.BlockSpec(memory_space=pltpu.VMEM)
    dma = pltpu.SemaphoreType.DMA
    slabs = (64, 16, 128)
    return pl.pallas_call(
        embed_kernel,
        out_shape=jax.ShapeDtypeStruct((8, 2, 24, 2048), jnp.bfloat16),
        in_specs=[vmem, vmem, vmem],
        out_specs=vmem,
        scratch_shapes=[
            pltpu.VMEM((VOCAB_PART // 128 * 128 + 128, 128), jnp.float32),
            pltpu.VMEM((64, 2, 128), jnp.int32),
            pltpu.VMEM((64, 2, 128), jnp.int32),
            pltpu.SMEM((64, 2, 128), jnp.int32),
            pltpu.VMEM((2, 16, 128), jnp.float32),
            pltpu.VMEM((2, 16, 128), jnp.float32),
            pltpu.VMEM((4,) + slabs, jnp.bfloat16),
            pltpu.VMEM((4,) + slabs, jnp.bfloat16),
            pltpu.VMEM((4,) + slabs, jnp.bfloat16),
            pltpu.VMEM((3,) + slabs, jnp.bfloat16),
            pltpu.VMEM(slabs, jnp.bfloat16),
            pltpu.VMEM(slabs, jnp.bfloat16),
            pltpu.VMEM((24, 4096), jnp.float32),
            pltpu.VMEM((2, 24, 2048), jnp.bfloat16),
            dma((64,)), dma((64,)), dma,
            dma((4,)), dma((4,)), dma((3,)), dma((3,)),
            dma((64,)), dma((64,)),
            dma((2,)), dma((2,)), dma((2,)), dma((2,)), dma((4,)), dma((4,)),
        ],
        compiler_params=pltpu.CompilerParams(
            collective_id=0, has_side_effects=True, vmem_limit_bytes=VMEM_LIMIT),
        name="look_up_scatter_norm",
    )(ids, table, gain)


def shards(token_ids, embed_table, input_gain, w_qkv, q_gain, k_gain):
    context_rank = lax.axis_index("context")
    local_len = token_ids.shape[1]
    w_all = lax.all_gather(w_qkv, "context", axis=0, tiled=True)
    ids = jnp.pad(token_ids, ((0, 0), (0, 128 - local_len)))
    normed = embed(ids, embed_table, input_gain[None])
    positions = context_rank * local_len + jnp.arange(local_len, dtype=jnp.int32)
    cos_t, sin_t = rope_tables(positions, HD)
    sin_t = jnp.concatenate([-sin_t[:, :64], sin_t[:, 64:]], axis=-1)
    return attention(normed, w_all, cos_t, sin_t, q_gain[None], k_gain[None])


def solution(mesh):
    return jax.shard_map(
        shards,
        mesh=mesh,
        in_specs=(P(None, "context"), P("context", "tensor"), P(), P("context", "tensor"), P(), P()),
        out_specs=P("context", "tensor", None),
        check_vma=False,
    )
```

```python
import functools

import jax
import jax.numpy as jnp
from jax import lax
from jax.experimental import pallas as pl
from jax.experimental.pallas import tpu as pltpu
from jax.sharding import PartitionSpec as P

QH = 32
KVH = 8
HD = 128
ROPE_BASE = 1000000.0
EPSILON = 1e-06
NEGATIVE = -1e30
MESH = pl.DeviceIdType.MESH
VMEM_LIMIT = 60 * 1024 * 1024


def rope_tables(positions, width):
    half_width = width // 2
    exponent = jnp.arange(half_width, dtype=jnp.float32) * (2.0 / width)
    inverse = jnp.exp(-exponent * jnp.log(jnp.float32(ROPE_BASE)))
    angles = positions.astype(jnp.float32)[:, None] * inverse[None, :]
    angles = jnp.concatenate([angles, angles], axis=-1)
    return (jnp.cos(angles), jnp.sin(angles))


def remote(src, dst, send_sem, recv_sem, t, c):
    return pltpu.make_async_remote_copy(
        src_ref=src, dst_ref=dst, send_sem=send_sem, recv_sem=recv_sem,
        device_id=(t, c), device_id_type=MESH)


def greet(barrier, t, c, me_t, me_c):
    own = jnp.logical_and(t == me_t, c == me_c)

    @pl.when(jnp.logical_not(own))
    def _():
        pl.semaphore_signal(barrier, inc=1, device_id=(t, c), device_id_type=MESH)

    return own.astype(jnp.int32)


K0 = 8
V0 = 72
W_CHUNKS = 8


def attention_kernel(x_ref, w_hbm, cos_ref, sin_ref, qg_ref, kg_ref, o_ref,
                     w_buf, acc_ref, heads, blocks, w_sem,
                     s1_send, s1_recv, s2_send, s2_recv, s3_send, s3_recv,
                     s4_send, s4_recv, max_ref, total_ref, sum_ref):
    t = lax.axis_index("tensor")
    c = lax.axis_index("context")
    x, k = t // 2, t % 2
    chunk = w_buf.shape[1]
    w_copies = [
        pltpu.make_async_copy(w_hbm.at[pl.ds(i * chunk, chunk)], w_buf.at[i], w_sem.at[i])
        for i in range(W_CHUNKS)
    ]
    for w_copy in w_copies:
        w_copy.start()

    head_u = c % QH
    group_u = head_u // 4
    y4 = head_u % 4
    barrier = pltpu.get_barrier_semaphore()
    kept = jnp.int32(0)
    for i in range(8):
        kept += greet(barrier, head_u // 6, 8 * t + i, t, c)
    for i in range(2):
        kept += greet(barrier, (QH + group_u) // 6, 8 * t + 2 * y4 + i, t, c)
        kept += greet(barrier, (QH + KVH + group_u) // 6, 8 * t + 2 * y4 + i, t, c)
    for d in range(1, 4):
        pl.semaphore_signal(barrier, inc=1, device_id=(t, c - y4 + (y4 + d) % 4), device_id_type=MESH)
    for d in range(1, 8):
        pl.semaphore_signal(barrier, inc=1, device_id=((t + d) % 8, c), device_id_type=MESH)

    for i in range(W_CHUNKS):
        w_copies[i].wait()
        at = i % 4 * chunk
        lhs = x_ref[:, i // 4, :, at:at + chunk].reshape(192, chunk)
        part = jnp.dot(lhs, w_buf[i], preferred_element_type=jnp.float32)
        if i == 0:
            acc_ref[...] = part
        else:
            acc_ref[...] += part

    cos_t, sin_t = cos_ref[...], sin_ref[...]
    for j in range(6):
        head = 6 * t + j
        gain = jnp.where(head < QH, qg_ref[...], kg_ref[...])
        for s in range(2):
            raw = acc_ref[96 * s:96 * s + 96, 128 * j:128 * j + 128].astype(jnp.bfloat16)
            wide = raw.astype(jnp.float32)
            mean_sq = jnp.mean(wide * wide, axis=-1, keepdims=True)
            scaled = wide * lax.rsqrt(mean_sq + EPSILON) * gain
            turned = scaled * cos_t + pltpu.roll(scaled, 64, 1) * sin_t
            heads[6 * s + j] = jnp.where(head < QH + KVH, turned, wide).astype(jnp.bfloat16)

    pl.semaphore_wait(barrier, 22 - kept)

    def stage1(b, start):
        s, j = b // 6, b % 6
        head = 6 * t + j
        is_q = head < QH
        i = jnp.maximum(head - QH, 0)
        kind, group = i // KVH, i % KVH
        to_c = s * QH + jnp.where(is_q, head, 4 * group + (c % 8) // 2)
        to_t = c // 8
        slot = jnp.where(is_q, c % 8, K0 + 64 * kind + c)
        sem = jnp.where(is_q, c % 8, 8 + 2 * kind + c % 2)
        own = jnp.logical_and(to_t == t, to_c == c)
        far = remote(heads.at[b], blocks.at[slot], s1_send.at[b], s1_recv.at[sem], to_t, to_c)

        @pl.when(own)
        def _():
            if start:
                pltpu.make_async_copy(heads.at[b], blocks.at[slot], s1_recv.at[sem]).start()

        @pl.when(jnp.logical_not(own))
        def _():
            if start:
                far.start()
            else:
                far.wait_send()

    def land(dst, sem):
        pltpu.make_async_copy(dst, dst, sem).wait()

    for b in range(12):
        stage1(b, True)
    base = 8 * t + 2 * y4
    for i in range(2):
        land(blocks.at[K0 + base + i], s1_recv.at[8 + i])
        land(blocks.at[V0 + base + i], s1_recv.at[10 + i])

    def stage2(kind, d):
        first = (K0, V0)[kind] + base
        peer = (y4 + d) % 4
        return remote(blocks.at[pl.ds(first, 2)], blocks.at[pl.ds(first, 2)],
                      s2_send.at[kind, d], s2_recv.at[kind, y4], t, c - y4 + peer)

    for kind in range(2):
        for d in range(1, 4):
            stage2(kind, d).start()
    for kind in range(2):
        for d in range(1, 4):
            peer = (y4 + d) % 4
            land(blocks.at[pl.ds((K0, V0)[kind] + 8 * t + 2 * peer, 2)], s2_recv.at[kind, peer])

    def slab(kind, tt):
        return blocks.at[pl.ds((K0, V0)[kind] + 8 * tt, 8)]

    def along_x(kind, of, to, n):
        return remote(slab(kind, 2 * of + k), slab(kind, 2 * of + k),
                      s3_send.at[n], s3_recv.at[kind, of], 2 * to + k, c)

    def arrived_x(kind, of):
        land(slab(kind, 2 * of + k), s3_recv.at[kind, of])

    def across(kind, of):
        return remote(slab(kind, 2 * of + k), slab(kind, 2 * of + k),
                      s4_send.at[kind, of], s4_recv.at[kind, of], 2 * x + 1 - k, c)

    def across_here(kind, of):
        last = jnp.where(k == 0, x, x - 1)
        return of <= last

    def hand_on(kind, of):
        @pl.when(across_here(kind, of))
        def _():
            across(kind, of).start()

    own_list = {
        0: [(0, 0, 1), (1, 0, 1), (0, 0, 3), (1, 0, 3)],
        1: [(1, 1, 0), (0, 1, 2), (1, 1, 2)],
        2: [(0, 2, 3), (1, 2, 3)],
        3: [],
    }
    relay_list = {0: [(1, 1, 3)], 1: [(0, 0, 2)], 2: [(0, 1, 3)], 3: [(1, 0, 2)]}
    get_list = {
        0: [],
        1: [(0, 0), (1, 0)],
        2: [(0, 1), (1, 1), (0, 0), (1, 0)],
        3: [(1, 0), (0, 0), (0, 2), (1, 2), (0, 1), (1, 1)],
    }
    for xx in range(4):
        @pl.when(x == xx)
        def _(xx=xx):
            for n, (kind, of, to) in enumerate(own_list[xx]):
                along_x(kind, of, to, n).start()
            for kind in range(2):
                @pl.when(k == 0)
                def _():
                    across(kind, xx).start()

    score_scale = HD ** (-0.5)
    rows = 256

    def update(state, q, keys, vals, mask):
        old_max, old_total, old_acc = state
        scores = lax.dot_general(q, keys, (((1,), (1,)), ((), ())),
                                 preferred_element_type=jnp.float32) * score_scale
        if mask is not None:
            scores = jnp.where(mask, scores, NEGATIVE)
        new_max = jnp.maximum(old_max, jnp.max(scores, axis=-1, keepdims=True))
        weights = jnp.exp(scores - new_max)
        shrink = jnp.exp(old_max - new_max)
        new_total = old_total * shrink + jnp.sum(weights, axis=-1, keepdims=True)
        new_acc = old_acc * shrink + jnp.dot(
            weights.astype(jnp.bfloat16), vals, preferred_element_type=jnp.float32)
        return new_max, new_total, new_acc

    for i in range(8):
        land(blocks.at[i], s1_recv.at[i])
    for i in range(3):
        q = blocks[0:8].reshape(768, HD)[rows * i:rows * (i + 1)]
        width = rows * (i + 1)
        keys = blocks[pl.ds(K0 + 8 * t, 8)].reshape(768, HD)[:width]
        vals = blocks[pl.ds(V0 + 8 * t, 8)].reshape(768, HD)[:width]
        mask = (lax.broadcasted_iota(jnp.int32, (rows, width), 1)
                <= lax.broadcasted_iota(jnp.int32, (rows, width), 0) + rows * i)
        state = (jnp.full((rows, 1), NEGATIVE, jnp.float32),
                 jnp.zeros((rows, 1), jnp.float32),
                 jnp.zeros((rows, HD), jnp.float32))
        max_ref[i], total_ref[i], sum_ref[i] = update(state, q, keys, vals, mask)

    def attend(i, first, count):
        q = blocks[0:8].reshape(768, HD)[rows * i:rows * (i + 1)]

        def step(of, state):
            keys = blocks[pl.ds(K0 + 8 * (2 * of + first), 8)].reshape(768, HD)
            vals = blocks[pl.ds(V0 + 8 * (2 * of + first), 8)].reshape(768, HD)
            return update(state, q, keys, vals, None)

        return lax.fori_loop(0, count, step, (max_ref[i], total_ref[i], sum_ref[i]))

    for xx in range(4):
        @pl.when(x == xx)
        def _(xx=xx):
            done = set()
            for n, (kind, of, to) in enumerate(relay_list[xx]):
                arrived_x(kind, of)
                done.add((kind, of))
                along_x(kind, of, to, len(own_list[xx]) + n).start()
                if of < xx:
                    across(kind, of).start()
            for kind, of in get_list[xx]:
                if (kind, of) not in done:
                    arrived_x(kind, of)
                    across(kind, of).start()

    for i in range(3):
        max_ref[i], total_ref[i], sum_ref[i] = attend(i, k, x)

    for of in range(4):
        for kind in range(2):
            @pl.when(jnp.where(k == 1, of <= x, of < x))
            def _():
                land(slab(kind, 2 * of + 1 - k), s4_recv.at[kind, of])

    for i in range(3):
        _, total, acc = attend(i, 1 - k, x + k)
        o_ref[0, rows * i:rows * (i + 1), :] = (acc / total).astype(jnp.bfloat16)

    for b in range(12):
        stage1(b, False)
    for kind in range(2):
        for d in range(1, 4):
            stage2(kind, d).wait_send()
    for xx in range(4):
        @pl.when(x == xx)
        def _(xx=xx):
            sends = own_list[xx] + relay_list[xx]
            for n, (kind, of, to) in enumerate(sends):
                along_x(kind, of, to, n).wait_send()
    for of in range(4):
        for kind in range(2):
            @pl.when(across_here(kind, of))
            def _():
                across(kind, of).wait_send()


def attention(normed, w_all, cos_t, sin_t, q_gain, k_gain):
    vmem = pl.BlockSpec(memory_space=pltpu.VMEM)
    dma = pltpu.SemaphoreType.DMA
    return pl.pallas_call(
        attention_kernel,
        out_shape=jax.ShapeDtypeStruct((1, 768, HD), jnp.bfloat16),
        in_specs=[vmem, pl.BlockSpec(memory_space=pl.ANY), vmem, vmem, vmem, vmem],
        out_specs=vmem,
        scratch_shapes=[
            pltpu.VMEM((W_CHUNKS, 4096 // W_CHUNKS, 768), jnp.bfloat16),
            pltpu.VMEM((192, 768), jnp.float32),
            pltpu.VMEM((12, 96, HD), jnp.bfloat16),
            pltpu.VMEM((136, 96, HD), jnp.bfloat16),
            dma((W_CHUNKS,)),
            dma((12,)), dma((12,)),
            dma((2, 4)), dma((2, 4)),
            dma((6,)), dma((2, 4)),
            dma((2, 4)), dma((2, 4)),
            pltpu.VMEM((3, 256, 1), jnp.float32),
            pltpu.VMEM((3, 256, 1), jnp.float32),
            pltpu.VMEM((3, 256, HD), jnp.float32),
        ],
        compiler_params=pltpu.CompilerParams(
            collective_id=1, has_side_effects=True, vmem_limit_bytes=VMEM_LIMIT),
        name="project_exchange_attend",
    )(normed, w_all, cos_t, sin_t, q_gain, k_gain)


VOCAB_PART = 18992
ZERO_ROW = VOCAB_PART


def embed_kernel(ids_ref, table_ref, gain_ref, w_ref, out_ref, w_out,
                 rows_ref, ids_v, ids_t, ids_s, pairs,
                 for_other, own, from_other, from_x, summed, pieces, wide_ref, normed,
                 ids_send, ids_recv, idx_sem, rs4_send, rs4_recv, rsx_send, rsx_recv,
                 a2a_send, a2a_recv, agx_send, agx_recv, agr_send, agr_recv, agp_send, agp_recv,
                 w_send, w_recv, w_sem):
    t = lax.axis_index("tensor")
    c = lax.axis_index("context")
    z, y = c // 8, c % 8
    keep_w = pltpu.make_async_copy(w_ref, w_out.at[z, y], w_sem)
    keep_w.start()
    x, k = t // 2, t % 2
    other = 2 * x + 1 - k
    barrier = pltpu.get_barrier_semaphore()

    @pl.loop(1, 64)
    def _(i):
        pl.semaphore_signal(barrier, inc=1, device_id=(t, (c + i) % 64), device_id_type=MESH)

    for d in range(1, 8):
        pl.semaphore_signal(barrier, inc=1, device_id=((t + d) % 8, c), device_id_type=MESH)

    def transpose(block):
        wide = block.astype(jnp.float32)
        return jnp.concatenate([wide, wide], axis=0).T

    full = VOCAB_PART // 128

    def turn(first, last):
        @pl.loop(first, last, unroll=2)
        def _(b):
            at = pl.multiple_of(b * 128, 128)
            rows_ref[pl.ds(at, 128), :] = transpose(table_ref[:, pl.ds(at, 128)])

    turn(0, full // 2)
    pl.semaphore_wait(barrier, 70)

    def land(dst, sem):
        pltpu.make_async_copy(dst, dst, sem).wait()

    def send_ids(i):
        return remote(ids_ref, ids_v.at[c], ids_send.at[i], ids_recv.at[c], t, (c + i) % 64)

    @pl.loop(1, 64)
    def _(i):
        send_ids(i).start()

    def w_block(stage, half, at):
        if (stage == 0) == (half == 0):
            return w_out.at[z, at, 0] if half == 0 else w_out.at[pl.ds(0, 8), at, 1]
        return w_out.at[at, pl.ds(0, 8), 0] if half == 0 else w_out.at[at, y, 1]

    def w_step(stage, half, up, step):
        here = y if (stage == 0) == (half == 0) else z
        sign = 1 if up else -1
        block = w_block(stage, half, (here - sign * step) % 8)
        to = (here + sign) % 8
        peer = 8 * z + to if (stage == 0) == (half == 0) else 8 * to + y
        n = step if up else 4 + step

        def copy():
            return remote(w_ref.at[half] if (stage, step) == (0, 0) else block, block,
                          w_send.at[stage, half, n], w_recv.at[stage, half, n], t, peer)

        return copy, w_block(stage, half, (here - sign * (step + 1)) % 8), w_recv.at[stage, half, n]

    w_rings = [(half, up) for half in range(2) for up in (True, False)]

    def pump(n):
        for step, starting in ((n - 1, False), (n, True)):
            stage, at = step // 4, step % 4
            if not 0 <= stage < 2:
                continue
            for half, up in w_rings:
                if at < (4 if up else 3):
                    copy, arriving, sem = w_step(stage, half, up, at)
                    if starting:
                        copy().start()
                    else:
                        land(arriving, sem)

    pump(0)
    ids_v[c] = ids_ref[...]
    turn(full // 2, full)
    rest = VOCAB_PART - full * 128
    tail = jnp.concatenate(
        [table_ref[:, full * 128:].astype(jnp.float32), jnp.zeros((64, 128 - rest), jnp.float32)], axis=1)
    rows_ref[full * 128:, :] = transpose(tail)

    pump(1)

    @pl.loop(1, 64)
    def _(i):
        src = (c + i) % 64
        land(ids_v.at[src], ids_recv.at[src])

    pump(2)

    for s in range(2):
        local = ids_v[:, s, :] - t * VOCAB_PART
        local = jnp.where(jnp.logical_and(local >= 0, local < VOCAB_PART), local, ZERO_ROW)
        for q in range(4):
            ids_t[4 * s + q] = pltpu.roll(local, 128 - 24 * q, 1) if q else local

    def to_smem(tp):
        return pltpu.make_async_copy(ids_t.at[tp], ids_s.at[tp], idx_sem.at[tp])

    for d in (2, 1, 3, 0):
        for kk in (1 - k, k):
            to_smem(2 * ((x + d) % 4) + kk).start()
    keep_w.wait()

    first_half = lax.broadcasted_iota(jnp.int32, (16, 128), 1) < 64

    def look_up(tp, dst, n):
        to_smem(tp).wait()

        @pl.loop(0, 32)
        def _(half):
            for m in range(2):
                cc = 2 * half + m
                for i in range(12):
                    first = rows_ref[pl.ds(ids_s[tp, cc, i], 1), :]
                    second = rows_ref[pl.ds(ids_s[tp, cc, 12 + i], 1), :]
                    pairs[m, i:i + 1, :] = jnp.where(first_half[:1], first, second)
            for m in range(2):
                dst[n, 2 * half + m] = pairs[m].astype(jnp.bfloat16)

    pairs[...] = jnp.zeros_like(pairs)

    def to_other(n):
        return remote(for_other.at[n], from_other.at[n], rs4_send.at[n], rs4_recv.at[n], other, c)

    def to_chip(n, xx):
        return remote(own.at[n], from_x.at[n], rsx_send.at[n], rsx_recv.at[n], 2 * xx + k, c)

    for n, d in enumerate((2, 1, 3, 0)):
        xx = (x + d) % 4
        look_up(2 * xx + 1 - k, for_other, n)
        to_other(n).start()
        if n < 2:
            pump(3 + n)
        look_up(2 * xx + k, own, n)
        land(from_other.at[n], rs4_recv.at[n])
        own[n] = own[n] + from_other[n]
        if d:
            to_chip(n, xx).start()

    for n in range(3):
        land(from_x.at[n], rsx_recv.at[n])
    summed[...] = (own[3] + from_x[0]) + (from_x[1] + from_x[2])

    def send_rows(i):
        peer = (c + i) % 64
        return remote(summed.at[peer], pieces.at[c], a2a_send.at[i], a2a_recv.at[c], t, peer)

    @pl.loop(1, 64)
    def _(i):
        send_rows(i).start()

    pieces[c] = summed[c]
    pump(5)

    @pl.loop(1, 64)
    def _(i):
        src = (c + i) % 64
        land(pieces.at[src], a2a_recv.at[src])

    pump(6)

    def add_squares(i, acc):
        piece = pieces[i].astype(jnp.float32)
        return acc + piece * piece

    squares = lax.fori_loop(0, 64, add_squares, jnp.zeros((16, 128), jnp.float32))
    sum_low = jnp.sum(jnp.where(first_half, squares, 0.0), axis=-1, keepdims=True)
    sum_high = jnp.sum(jnp.where(first_half, 0.0, squares), axis=-1, keepdims=True)
    scale_low = lax.rsqrt(sum_low / 4096 + EPSILON)
    scale_high = lax.rsqrt(sum_high / 4096 + EPSILON)
    for p in range(32):
        even = pieces[2 * p].astype(jnp.float32)
        odd = pieces[2 * p + 1].astype(jnp.float32)
        gain = gain_ref[:, 128 * p:128 * p + 128]
        low_rows = jnp.where(first_half, even, pltpu.roll(odd, 64, 1)) * scale_low * gain
        high_rows = jnp.where(first_half, pltpu.roll(even, 64, 1), odd) * scale_high * gain
        wide_ref[0:12, 128 * p:128 * p + 128] = low_rows[:12]
        wide_ref[12:24, 128 * p:128 * p + 128] = high_rows[:12]
    for h in range(2):
        part = wide_ref[:, 2048 * h:2048 * h + 2048].astype(jnp.bfloat16)
        normed[h] = part
        out_ref[t, h] = part

    right, left = 2 * ((x + 1) % 4) + k, 2 * ((x + 3) % 4) + k
    across = 2 * ((x + 2) % 4) + k
    to_right = remote(normed, out_ref.at[t], agx_send.at[0], agx_recv.at[0], right, c)
    to_left = remote(normed, out_ref.at[t], agx_send.at[1], agx_recv.at[1], left, c)
    to_right.start()
    to_left.start()

    def hand_over(src, tt, n):
        return remote(src, out_ref.at[tt], agp_send.at[n], agp_recv.at[n], other, c)

    hand_own = hand_over(normed, t, 0)
    hand_own.start()
    land(out_ref.at[left], agx_recv.at[0])
    on_right = remote(out_ref.at[left, 0], out_ref.at[left, 0], agr_send.at[0], agr_recv.at[0], right, c)
    on_right.start()
    hand_left = hand_over(out_ref.at[left], left, 1)
    hand_left.start()
    land(out_ref.at[right], agx_recv.at[1])
    on_left = remote(out_ref.at[right, 1], out_ref.at[right, 1], agr_send.at[1], agr_recv.at[1], left, c)
    on_left.start()
    hand_right = hand_over(out_ref.at[right], right, 2)
    hand_right.start()
    land(out_ref.at[across, 0], agr_recv.at[0])
    land(out_ref.at[across, 1], agr_recv.at[1])
    hand_across = hand_over(out_ref.at[across], across, 3)
    hand_across.start()
    pump(7)

    flip = 1 - 2 * k
    land(out_ref.at[t + flip], agp_recv.at[0])
    land(out_ref.at[left + flip], agp_recv.at[1])
    land(out_ref.at[right + flip], agp_recv.at[2])
    land(out_ref.at[across + flip], agp_recv.at[3])

    pump(8)
    for stage in range(2):
        for half, up in w_rings:
            for step in range(4 if up else 3):
                w_step(stage, half, up, step)[0]().wait_send()

    @pl.loop(1, 64)
    def _(i):
        send_ids(i).wait_send()
        send_rows(i).wait_send()

    for n, d in enumerate((2, 1, 3, 0)):
        to_other(n).wait_send()
        if d:
            to_chip(n, (x + d) % 4).wait_send()
    for copy in (to_right, to_left, on_right, on_left, hand_own, hand_left, hand_right, hand_across):
        copy.wait_send()


def embed(ids, table, gain, w_part):
    vmem = pl.BlockSpec(memory_space=pltpu.VMEM)
    dma = pltpu.SemaphoreType.DMA
    slabs = (64, 16, 128)
    return pl.pallas_call(
        embed_kernel,
        out_shape=(jax.ShapeDtypeStruct((8, 2, 24, 2048), jnp.bfloat16),
                   jax.ShapeDtypeStruct((8, 8, 2, 32, 768), jnp.bfloat16)),
        in_specs=[vmem, vmem, vmem, vmem],
        out_specs=(vmem, pl.BlockSpec(memory_space=pl.ANY)),
        scratch_shapes=[
            pltpu.VMEM((VOCAB_PART // 128 * 128 + 128, 128), jnp.float32),
            pltpu.VMEM((64, 2, 128), jnp.int32),
            pltpu.VMEM((8, 64, 128), jnp.int32),
            pltpu.SMEM((8, 64, 128), jnp.int32),
            pltpu.VMEM((2, 16, 128), jnp.float32),
            pltpu.VMEM((4,) + slabs, jnp.bfloat16),
            pltpu.VMEM((4,) + slabs, jnp.bfloat16),
            pltpu.VMEM((4,) + slabs, jnp.bfloat16),
            pltpu.VMEM((3,) + slabs, jnp.bfloat16),
            pltpu.VMEM(slabs, jnp.bfloat16),
            pltpu.VMEM(slabs, jnp.bfloat16),
            pltpu.VMEM((24, 4096), jnp.float32),
            pltpu.VMEM((2, 24, 2048), jnp.bfloat16),
            dma((64,)), dma((64,)), dma((8,)),
            dma((4,)), dma((4,)), dma((3,)), dma((3,)),
            dma((64,)), dma((64,)),
            dma((2,)), dma((2,)), dma((2,)), dma((2,)), dma((4,)), dma((4,)),
            dma((2, 2, 7)), dma((2, 2, 7)), dma,
        ],
        compiler_params=pltpu.CompilerParams(
            collective_id=0, has_side_effects=True, vmem_limit_bytes=VMEM_LIMIT),
        name="look_up_scatter_norm",
    )(ids, table, gain, w_part)


def shards(token_ids, embed_table, input_gain, w_qkv, q_gain, k_gain):
    context_rank = lax.axis_index("context")
    local_len = token_ids.shape[1]
    ids = jnp.pad(token_ids, ((0, 0), (0, 128 - local_len)))
    normed, w_all = embed(ids, embed_table, input_gain[None], w_qkv.reshape(2, 32, -1))
    w_all = w_all.reshape(4096, -1)
    positions = context_rank * local_len + jnp.arange(local_len, dtype=jnp.int32)
    cos_t, sin_t = rope_tables(positions, HD)
    sin_t = jnp.concatenate([-sin_t[:, :64], sin_t[:, 64:]], axis=-1)
    return attention(normed, w_all, cos_t, sin_t, q_gain[None], k_gain[None])


def solution(mesh):
    return jax.shard_map(
        shards,
        mesh=mesh,
        in_specs=(P(None, "context"), P("context", "tensor"), P(), P("context", "tensor"), P(), P()),
        out_specs=P("context", "tensor", None),
        check_vma=False,
    )
```

```python
import functools

import jax
import jax.numpy as jnp
from jax import lax
from jax.experimental import pallas as pl
from jax.experimental.pallas import tpu as pltpu
from jax.sharding import PartitionSpec as P

QH = 32
KVH = 8
HD = 128
ROPE_BASE = 1000000.0
EPSILON = 1e-06
NEGATIVE = -1e30
MESH = pl.DeviceIdType.MESH
VMEM_LIMIT = 60 * 1024 * 1024


def rope_tables(positions, width):
    half_width = width // 2
    exponent = jnp.arange(half_width, dtype=jnp.float32) * (2.0 / width)
    inverse = jnp.exp(-exponent * jnp.log(jnp.float32(ROPE_BASE)))
    angles = positions.astype(jnp.float32)[:, None] * inverse[None, :]
    angles = jnp.concatenate([angles, angles], axis=-1)
    return (jnp.cos(angles), jnp.sin(angles))


def remote(src, dst, send_sem, recv_sem, t, c):
    return pltpu.make_async_remote_copy(
        src_ref=src, dst_ref=dst, send_sem=send_sem, recv_sem=recv_sem,
        device_id=(t, c), device_id_type=MESH)


def greet(barrier, t, c, me_t, me_c):
    own = jnp.logical_and(t == me_t, c == me_c)

    @pl.when(jnp.logical_not(own))
    def _():
        pl.semaphore_signal(barrier, inc=1, device_id=(t, c), device_id_type=MESH)

    return own.astype(jnp.int32)


def group_of(c):
    return 8 * ((c // 8 + c % 8) % 8) + c % 8


def holder_of(g):
    return 8 * ((g // 8 - g % 8 + 8) % 8) + g % 8


K0 = 8
V0 = 72
W_CHUNKS = 8


def attention_kernel(x_ref, w_hbm, cos_ref, sin_ref, qg_ref, kg_ref, o_ref,
                     w_buf, acc_ref, heads, blocks, w_sem,
                     s1_send, s1_recv, s2_send, s2_recv, s3_send, s3_recv,
                     s4_send, s4_recv, max_ref, total_ref, sum_ref):
    t = lax.axis_index("tensor")
    c = lax.axis_index("context")
    x, k = t // 2, t % 2
    g = group_of(c)
    chunk = w_buf.shape[1]
    w_copies = [
        pltpu.make_async_copy(w_hbm.at[pl.ds(i * chunk, chunk)], w_buf.at[i], w_sem.at[i])
        for i in range(W_CHUNKS)
    ]
    for w_copy in w_copies:
        w_copy.start()

    head_u = c % QH
    group_u = head_u // 4
    y4 = head_u % 4
    barrier = pltpu.get_barrier_semaphore()
    kept = jnp.int32(0)
    for i in range(8):
        kept += greet(barrier, head_u // 6, holder_of(8 * t + i), t, c)
    for i in range(2):
        kept += greet(barrier, (QH + group_u) // 6, holder_of(8 * t + 2 * y4 + i), t, c)
        kept += greet(barrier, (QH + KVH + group_u) // 6, holder_of(8 * t + 2 * y4 + i), t, c)
    for d in range(1, 4):
        pl.semaphore_signal(barrier, inc=1, device_id=(t, c - y4 + (y4 + d) % 4), device_id_type=MESH)
    for d in range(1, 8):
        pl.semaphore_signal(barrier, inc=1, device_id=((t + d) % 8, c), device_id_type=MESH)

    for i in range(W_CHUNKS):
        w_copies[i].wait()
        at = i % 4 * chunk
        lhs = x_ref[:, i // 4, :, at:at + chunk].reshape(192, chunk)
        part = jnp.dot(lhs, w_buf[i], preferred_element_type=jnp.float32)
        if i == 0:
            acc_ref[...] = part
        else:
            acc_ref[...] += part

    cos_t, sin_t = cos_ref[...], sin_ref[...]
    for j in range(6):
        head = 6 * t + j
        gain = jnp.where(head < QH, qg_ref[...], kg_ref[...])
        for s in range(2):
            raw = acc_ref[96 * s:96 * s + 96, 128 * j:128 * j + 128].astype(jnp.bfloat16)
            wide = raw.astype(jnp.float32)
            mean_sq = jnp.mean(wide * wide, axis=-1, keepdims=True)
            scaled = wide * lax.rsqrt(mean_sq + EPSILON) * gain
            turned = scaled * cos_t + pltpu.roll(scaled, 64, 1) * sin_t
            heads[6 * s + j] = jnp.where(head < QH + KVH, turned, wide).astype(jnp.bfloat16)

    pl.semaphore_wait(barrier, 22 - kept)

    def stage1(b, start):
        s, j = b // 6, b % 6
        head = 6 * t + j
        is_q = head < QH
        i = jnp.maximum(head - QH, 0)
        kind, group = i // KVH, i % KVH
        to_c = s * QH + jnp.where(is_q, head, 4 * group + (g % 8) // 2)
        to_t = g // 8
        slot = jnp.where(is_q, g % 8, K0 + 64 * kind + g)
        sem = jnp.where(is_q, g % 8, 8 + 2 * kind + g % 2)
        own = jnp.logical_and(to_t == t, to_c == c)
        far = remote(heads.at[b], blocks.at[slot], s1_send.at[b], s1_recv.at[sem], to_t, to_c)

        @pl.when(own)
        def _():
            if start:
                pltpu.make_async_copy(heads.at[b], blocks.at[slot], s1_recv.at[sem]).start()

        @pl.when(jnp.logical_not(own))
        def _():
            if start:
                far.start()
            else:
                far.wait_send()

    def land(dst, sem):
        pltpu.make_async_copy(dst, dst, sem).wait()

    for b in range(12):
        stage1(b, True)
    base = 8 * t + 2 * y4
    def stage2(kind, d):
        first = (K0, V0)[kind] + base
        peer = (y4 + d) % 4
        return remote(blocks.at[pl.ds(first, 2)], blocks.at[pl.ds(first, 2)],
                      s2_send.at[kind, d], s2_recv.at[kind, y4], t, c - y4 + peer)

    for kind in range(2):
        for i in range(2):
            land(blocks.at[(K0, V0)[kind] + base + i], s1_recv.at[8 + 2 * kind + i])
        for d in range(1, 4):
            stage2(kind, d).start()

    def slab(kind, tt):
        return blocks.at[pl.ds((K0, V0)[kind] + 8 * tt, 8)]

    def along_x(kind, of, to, n):
        return remote(slab(kind, 2 * of + k), slab(kind, 2 * of + k),
                      s3_send.at[n], s3_recv.at[kind, of], 2 * to + k, c)

    def arrived_x(kind, of):
        land(slab(kind, 2 * of + k), s3_recv.at[kind, of])

    def across(kind, of):
        return remote(slab(kind, 2 * of + k), slab(kind, 2 * of + k),
                      s4_send.at[kind, of], s4_recv.at[kind, of], 2 * x + 1 - k, c)

    def across_here(kind, of):
        last = jnp.where(k == 0, x, x - 1)
        return of <= last

    def hand_on(kind, of):
        @pl.when(across_here(kind, of))
        def _():
            across(kind, of).start()

    own_list = {
        0: [(0, 0, 1), (1, 0, 1), (0, 0, 3), (1, 0, 3)],
        1: [(1, 1, 0), (0, 1, 2), (1, 1, 2)],
        2: [(0, 2, 3), (1, 2, 3)],
        3: [],
    }
    relay_list = {0: [(1, 1, 3)], 1: [(0, 0, 2)], 2: [(0, 1, 3)], 3: [(1, 0, 2)]}
    get_list = {
        0: [],
        1: [(0, 0), (1, 0)],
        2: [(0, 1), (1, 1), (0, 0), (1, 0)],
        3: [(1, 0), (0, 0), (0, 2), (1, 2), (0, 1), (1, 1)],
    }
    for now in range(2):
        for d in range(1, 4):
            peer = (y4 + d) % 4
            land(blocks.at[pl.ds((K0, V0)[now] + 8 * t + 2 * peer, 2)], s2_recv.at[now, peer])
        for xx in range(4):
            @pl.when(x == xx)
            def _(xx=xx):
                for n, (kind, of, to) in enumerate(own_list[xx]):
                    if kind == now:
                        along_x(kind, of, to, n).start()

                @pl.when(k == 0)
                def _():
                    across(now, xx).start()

    score_scale = HD ** (-0.5)
    rows = 256

    def update(state, q, keys, vals, mask):
        old_max, old_total, old_acc = state
        scores = lax.dot_general(q, keys, (((1,), (1,)), ((), ())),
                                 preferred_element_type=jnp.float32) * score_scale
        if mask is not None:
            scores = jnp.where(mask, scores, NEGATIVE)
        new_max = jnp.maximum(old_max, jnp.max(scores, axis=-1, keepdims=True))
        weights = jnp.exp(scores - new_max)
        shrink = jnp.exp(old_max - new_max)
        new_total = old_total * shrink + jnp.sum(weights, axis=-1, keepdims=True)
        new_acc = old_acc * shrink + jnp.dot(
            weights.astype(jnp.bfloat16), vals, preferred_element_type=jnp.float32)
        return new_max, new_total, new_acc

    for i in range(8):
        land(blocks.at[i], s1_recv.at[i])
    for i in range(3):
        q = blocks[0:8].reshape(768, HD)[rows * i:rows * (i + 1)]
        width = rows * (i + 1)
        keys = blocks[pl.ds(K0 + 8 * t, 8)].reshape(768, HD)[:width]
        vals = blocks[pl.ds(V0 + 8 * t, 8)].reshape(768, HD)[:width]
        mask = (lax.broadcasted_iota(jnp.int32, (rows, width), 1)
                <= lax.broadcasted_iota(jnp.int32, (rows, width), 0) + rows * i)
        state = (jnp.full((rows, 1), NEGATIVE, jnp.float32),
                 jnp.zeros((rows, 1), jnp.float32),
                 jnp.zeros((rows, HD), jnp.float32))
        max_ref[i], total_ref[i], sum_ref[i] = update(state, q, keys, vals, mask)

    def attend(i, first, count):
        q = blocks[0:8].reshape(768, HD)[rows * i:rows * (i + 1)]

        def step(of, state):
            keys = blocks[pl.ds(K0 + 8 * (2 * of + first), 8)].reshape(768, HD)
            vals = blocks[pl.ds(V0 + 8 * (2 * of + first), 8)].reshape(768, HD)
            return update(state, q, keys, vals, None)

        return lax.fori_loop(0, count, step, (max_ref[i], total_ref[i], sum_ref[i]))

    for xx in range(4):
        @pl.when(x == xx)
        def _(xx=xx):
            done = set()
            for n, (kind, of, to) in enumerate(relay_list[xx]):
                arrived_x(kind, of)
                done.add((kind, of))
                along_x(kind, of, to, len(own_list[xx]) + n).start()
                if of < xx:
                    across(kind, of).start()
            for kind, of in get_list[xx]:
                if (kind, of) not in done:
                    arrived_x(kind, of)
                    across(kind, of).start()

    for i in range(3):
        max_ref[i], total_ref[i], sum_ref[i] = attend(i, k, x)

    for of in range(4):
        for kind in range(2):
            @pl.when(jnp.where(k == 1, of <= x, of < x))
            def _():
                land(slab(kind, 2 * of + 1 - k), s4_recv.at[kind, of])

    for i in range(3):
        _, total, acc = attend(i, 1 - k, x + k)
        o_ref[0, rows * i:rows * (i + 1), :] = (acc / total).astype(jnp.bfloat16)

    for b in range(12):
        stage1(b, False)
    for kind in range(2):
        for d in range(1, 4):
            stage2(kind, d).wait_send()
    for xx in range(4):
        @pl.when(x == xx)
        def _(xx=xx):
            sends = own_list[xx] + relay_list[xx]
            for n, (kind, of, to) in enumerate(sends):
                along_x(kind, of, to, n).wait_send()
    for of in range(4):
        for kind in range(2):
            @pl.when(across_here(kind, of))
            def _():
                across(kind, of).wait_send()


def attention(normed, w_all, cos_t, sin_t, q_gain, k_gain):
    vmem = pl.BlockSpec(memory_space=pltpu.VMEM)
    dma = pltpu.SemaphoreType.DMA
    return pl.pallas_call(
        attention_kernel,
        out_shape=jax.ShapeDtypeStruct((1, 768, HD), jnp.bfloat16),
        in_specs=[vmem, pl.BlockSpec(memory_space=pl.ANY), vmem, vmem, vmem, vmem],
        out_specs=vmem,
        scratch_shapes=[
            pltpu.VMEM((W_CHUNKS, 4096 // W_CHUNKS, 768), jnp.bfloat16),
            pltpu.VMEM((192, 768), jnp.float32),
            pltpu.VMEM((12, 96, HD), jnp.bfloat16),
            pltpu.VMEM((136, 96, HD), jnp.bfloat16),
            dma((W_CHUNKS,)),
            dma((12,)), dma((12,)),
            dma((2, 4)), dma((2, 4)),
            dma((6,)), dma((2, 4)),
            dma((2, 4)), dma((2, 4)),
            pltpu.VMEM((3, 256, 1), jnp.float32),
            pltpu.VMEM((3, 256, 1), jnp.float32),
            pltpu.VMEM((3, 256, HD), jnp.float32),
        ],
        compiler_params=pltpu.CompilerParams(
            collective_id=1, has_side_effects=True, vmem_limit_bytes=VMEM_LIMIT),
        name="project_exchange_attend",
    )(normed, w_all, cos_t, sin_t, q_gain, k_gain)


VOCAB_PART = 18992
ZERO_ROW = VOCAB_PART


def embed_kernel(ids_ref, table_ref, gain_ref, w_ref, out_ref, w_out,
                 rows_ref, id_row, ids_v, ids_t, ids_s, pairs,
                 for_other, own, from_other, from_x, summed, pieces, wide_ref, normed,
                 ids_send, ids_recv, idx_sem, rs4_send, rs4_recv, rsx_send, rsx_recv,
                 a2a_send, a2a_recv, agx_send, agx_recv, agr_send, agr_recv, agp_send, agp_recv,
                 w_send, w_recv, w_sem):
    t = lax.axis_index("tensor")
    c = lax.axis_index("context")
    z, y = c // 8, c % 8
    keep_w = pltpu.make_async_copy(w_ref, w_out.at[z, y], w_sem)
    keep_w.start()
    x, k = t // 2, t % 2
    other = 2 * x + 1 - k
    barrier = pltpu.get_barrier_semaphore()

    @pl.loop(1, 64)
    def _(i):
        pl.semaphore_signal(barrier, inc=1, device_id=(t, (c + i) % 64), device_id_type=MESH)

    for d in range(1, 8):
        pl.semaphore_signal(barrier, inc=1, device_id=((t + d) % 8, c), device_id_type=MESH)

    twice = (lax.broadcasted_iota(jnp.int32, (64, 128), 1) % 64
             == lax.broadcasted_iota(jnp.int32, (64, 128), 0)).astype(jnp.float32).astype(jnp.bfloat16)

    def transpose(block):
        return lax.dot_general(block, twice, (((0,), (0,)), ((), ())), preferred_element_type=jnp.float32)

    full = VOCAB_PART // 128

    def turn(first, last):
        @pl.loop(first, last, unroll=2)
        def _(b):
            at = pl.multiple_of(b * 128, 128)
            rows_ref[pl.ds(at, 128), :] = transpose(table_ref[:, pl.ds(at, 128)])

    id_row[...] = jnp.zeros_like(id_row)
    id_row[:, :ids_ref.shape[1]] = ids_ref[...]
    turn(0, 50)
    pl.semaphore_wait(barrier, 70)

    def land(dst, sem):
        pltpu.make_async_copy(dst, dst, sem).wait()

    def send_ids(i):
        return remote(id_row, ids_v.at[c], ids_send.at[i], ids_recv.at[c], t, (c + i) % 64)

    @pl.loop(1, 64)
    def _(i):
        send_ids(i).start()

    def w_block(stage, half, at):
        if (stage == 0) == (half == 0):
            return w_out.at[z, at, 0] if half == 0 else w_out.at[pl.ds(0, 8), at, 1]
        return w_out.at[at, pl.ds(0, 8), 0] if half == 0 else w_out.at[at, y, 1]

    def w_step(stage, half, up, step):
        here = y if (stage == 0) == (half == 0) else z
        sign = 1 if up else -1
        block = w_block(stage, half, (here - sign * step) % 8)
        to = (here + sign) % 8
        peer = 8 * z + to if (stage == 0) == (half == 0) else 8 * to + y
        n = step if up else 4 + step

        def copy():
            return remote(w_ref.at[half] if (stage, step) == (0, 0) else block, block,
                          w_send.at[stage, half, n], w_recv.at[stage, half, n], t, peer)

        return copy, w_block(stage, half, (here - sign * (step + 1)) % 8), w_recv.at[stage, half, n]

    w_rings = [(half, up) for half in range(2) for up in (True, False)]

    def pump(n):
        for step, starting in ((n - 1, False), (n, True)):
            stage, at = step // 4, step % 4
            if not 0 <= stage < 2:
                continue
            for half, up in w_rings:
                if at < (4 if up else 3):
                    copy, arriving, sem = w_step(stage, half, up, at)
                    if starting:
                        copy().start()
                    else:
                        land(arriving, sem)

    pump(0)
    ids_v[c] = id_row[...]
    turn(50, 84)
    pump(1)
    turn(84, 116)
    pump(2)
    turn(116, full)
    rest = VOCAB_PART - full * 128
    tail = jnp.concatenate(
        [table_ref[:, full * 128:].astype(jnp.float32), jnp.zeros((64, 128 - rest), jnp.float32)], axis=1)
    rows_ref[full * 128:, :] = transpose(tail.astype(jnp.bfloat16))

    pump(3)

    @pl.loop(1, 64)
    def _(i):
        src = (c + i) % 64
        land(ids_v.at[src], ids_recv.at[src])

    for s in range(2):
        local = ids_v[:, s, :] - t * VOCAB_PART
        local = jnp.where(jnp.logical_and(local >= 0, local < VOCAB_PART), local, ZERO_ROW)
        for q in range(4):
            ids_t[4 * s + q] = pltpu.roll(local, 128 - 24 * q, 1) if q else local

    def to_smem(tp):
        return pltpu.make_async_copy(ids_t.at[tp], ids_s.at[tp], idx_sem.at[tp])

    for d in (2, 1, 3, 0):
        for kk in (1 - k, k):
            to_smem(2 * ((x + d) % 4) + kk).start()
    keep_w.wait()
    pump(4)

    first_half = lax.broadcasted_iota(jnp.int32, (16, 128), 1) < 64

    def look_up(tp, dst, n):
        to_smem(tp).wait()

        @pl.loop(0, 32)
        def _(half):
            for m in range(2):
                cc = 2 * half + m
                for i in range(12):
                    first = rows_ref[pl.ds(ids_s[tp, cc, i], 1), :]
                    second = rows_ref[pl.ds(ids_s[tp, cc, 12 + i], 1), :]
                    pairs[m, i:i + 1, :] = jnp.where(first_half[:1], first, second)
            for m in range(2):
                dst[n, 2 * half + m] = pairs[m].astype(jnp.bfloat16)

    pairs[...] = jnp.zeros_like(pairs)

    def to_other(n):
        return remote(for_other.at[n], from_other.at[n], rs4_send.at[n], rs4_recv.at[n], other, c)

    def to_chip(n, xx):
        return remote(own.at[n], from_x.at[n], rsx_send.at[n], rsx_recv.at[n], 2 * xx + k, c)

    for n, d in enumerate((2, 1, 3, 0)):
        xx = (x + d) % 4
        look_up(2 * xx + 1 - k, for_other, n)
        to_other(n).start()
        if n == 2:
            pump(5)
        look_up(2 * xx + k, own, n)
        land(from_other.at[n], rs4_recv.at[n])
        own[n] = own[n] + from_other[n]
        if d:
            to_chip(n, xx).start()

    for n in range(3):
        land(from_x.at[n], rsx_recv.at[n])
    summed[...] = (own[3] + from_x[0]) + (from_x[1] + from_x[2])

    def send_rows(i):
        peer = (c + i) % 64
        return remote(summed.at[group_of(peer)], pieces.at[c], a2a_send.at[i], a2a_recv.at[c], t, peer)

    @pl.loop(1, 64)
    def _(i):
        send_rows(i).start()

    pieces[c] = summed[group_of(c)]
    pump(6)

    @pl.loop(1, 64)
    def _(i):
        src = (c + i) % 64
        land(pieces.at[src], a2a_recv.at[src])

    pump(7)

    def add_squares(i, acc):
        piece = pieces[i].astype(jnp.float32)
        return acc + piece * piece

    squares = lax.fori_loop(0, 64, add_squares, jnp.zeros((16, 128), jnp.float32))
    sum_low = jnp.sum(jnp.where(first_half, squares, 0.0), axis=-1, keepdims=True)
    sum_high = jnp.sum(jnp.where(first_half, 0.0, squares), axis=-1, keepdims=True)
    scale_low = lax.rsqrt(sum_low / 4096 + EPSILON)
    scale_high = lax.rsqrt(sum_high / 4096 + EPSILON)
    for p in range(32):
        even = pieces[2 * p].astype(jnp.float32)
        odd = pieces[2 * p + 1].astype(jnp.float32)
        gain = gain_ref[:, 128 * p:128 * p + 128]
        low_rows = jnp.where(first_half, even, pltpu.roll(odd, 64, 1)) * scale_low * gain
        high_rows = jnp.where(first_half, pltpu.roll(even, 64, 1), odd) * scale_high * gain
        wide_ref[0:12, 128 * p:128 * p + 128] = low_rows[:12]
        wide_ref[12:24, 128 * p:128 * p + 128] = high_rows[:12]
    for h in range(2):
        part = wide_ref[:, 2048 * h:2048 * h + 2048].astype(jnp.bfloat16)
        normed[h] = part
        out_ref[t, h] = part

    right, left = 2 * ((x + 1) % 4) + k, 2 * ((x + 3) % 4) + k
    across = 2 * ((x + 2) % 4) + k
    to_right = remote(normed, out_ref.at[t], agx_send.at[0], agx_recv.at[0], right, c)
    to_left = remote(normed, out_ref.at[t], agx_send.at[1], agx_recv.at[1], left, c)
    to_right.start()
    to_left.start()

    def hand_over(src, tt, n):
        return remote(src, out_ref.at[tt], agp_send.at[n], agp_recv.at[n], other, c)

    hand_own = hand_over(normed, t, 0)
    hand_own.start()
    land(out_ref.at[left], agx_recv.at[0])
    on_right = remote(out_ref.at[left, 0], out_ref.at[left, 0], agr_send.at[0], agr_recv.at[0], right, c)
    on_right.start()
    hand_left = hand_over(out_ref.at[left], left, 1)
    hand_left.start()
    land(out_ref.at[right], agx_recv.at[1])
    on_left = remote(out_ref.at[right, 1], out_ref.at[right, 1], agr_send.at[1], agr_recv.at[1], left, c)
    on_left.start()
    hand_right = hand_over(out_ref.at[right], right, 2)
    hand_right.start()
    land(out_ref.at[across, 0], agr_recv.at[0])
    land(out_ref.at[across, 1], agr_recv.at[1])
    hand_across = hand_over(out_ref.at[across], across, 3)
    hand_across.start()

    flip = 1 - 2 * k
    land(out_ref.at[t + flip], agp_recv.at[0])
    land(out_ref.at[left + flip], agp_recv.at[1])
    land(out_ref.at[right + flip], agp_recv.at[2])
    land(out_ref.at[across + flip], agp_recv.at[3])

    pump(8)
    for stage in range(2):
        for half, up in w_rings:
            for step in range(4 if up else 3):
                w_step(stage, half, up, step)[0]().wait_send()

    @pl.loop(1, 64)
    def _(i):
        send_ids(i).wait_send()
        send_rows(i).wait_send()

    for n, d in enumerate((2, 1, 3, 0)):
        to_other(n).wait_send()
        if d:
            to_chip(n, (x + d) % 4).wait_send()
    for copy in (to_right, to_left, on_right, on_left, hand_own, hand_left, hand_right, hand_across):
        copy.wait_send()


def embed(ids, table, gain, w_part):
    vmem = pl.BlockSpec(memory_space=pltpu.VMEM)
    dma = pltpu.SemaphoreType.DMA
    slabs = (64, 16, 128)
    return pl.pallas_call(
        embed_kernel,
        out_shape=(jax.ShapeDtypeStruct((8, 2, 24, 2048), jnp.bfloat16),
                   jax.ShapeDtypeStruct((8, 8, 2, 32, 768), jnp.bfloat16)),
        in_specs=[vmem, vmem, vmem, vmem],
        out_specs=(vmem, pl.BlockSpec(memory_space=pl.ANY)),
        scratch_shapes=[
            pltpu.VMEM((VOCAB_PART // 128 * 128 + 128, 128), jnp.float32),
            pltpu.VMEM((2, 128), jnp.int32),
            pltpu.VMEM((64, 2, 128), jnp.int32),
            pltpu.VMEM((8, 64, 128), jnp.int32),
            pltpu.SMEM((8, 64, 128), jnp.int32),
            pltpu.VMEM((2, 16, 128), jnp.float32),
            pltpu.VMEM((4,) + slabs, jnp.bfloat16),
            pltpu.VMEM((4,) + slabs, jnp.bfloat16),
            pltpu.VMEM((4,) + slabs, jnp.bfloat16),
            pltpu.VMEM((3,) + slabs, jnp.bfloat16),
            pltpu.VMEM(slabs, jnp.bfloat16),
            pltpu.VMEM(slabs, jnp.bfloat16),
            pltpu.VMEM((24, 4096), jnp.float32),
            pltpu.VMEM((2, 24, 2048), jnp.bfloat16),
            dma((64,)), dma((64,)), dma((8,)),
            dma((4,)), dma((4,)), dma((3,)), dma((3,)),
            dma((64,)), dma((64,)),
            dma((2,)), dma((2,)), dma((2,)), dma((2,)), dma((4,)), dma((4,)),
            dma((2, 2, 7)), dma((2, 2, 7)), dma,
        ],
        compiler_params=pltpu.CompilerParams(
            collective_id=0, has_side_effects=True, vmem_limit_bytes=VMEM_LIMIT),
        name="look_up_scatter_norm",
    )(ids, table, gain, w_part)


def shards(token_ids, embed_table, input_gain, w_qkv, q_gain, k_gain):
    context_rank = lax.axis_index("context")
    local_len = token_ids.shape[1]
    normed, w_all = embed(token_ids, embed_table, input_gain[None], w_qkv.reshape(2, 32, -1))
    w_all = w_all.reshape(4096, -1)
    positions = group_of(context_rank) * local_len + jnp.arange(local_len, dtype=jnp.int32)
    cos_t, sin_t = rope_tables(positions, HD)
    sin_t = jnp.concatenate([-sin_t[:, :64], sin_t[:, 64:]], axis=-1)
    return attention(normed, w_all, cos_t, sin_t, q_gain[None], k_gain[None])


def solution(mesh):
    return jax.shard_map(
        shards,
        mesh=mesh,
        in_specs=(P(None, "context"), P("context", "tensor"), P(), P("context", "tensor"), P(), P()),
        out_specs=P("context", "tensor", None),
        check_vma=False,
    )
```

```python
import functools

import jax
import jax.numpy as jnp
from jax import lax
from jax.experimental import pallas as pl
from jax.experimental.pallas import tpu as pltpu
from jax.sharding import PartitionSpec as P

QH = 32
KVH = 8
HD = 128
ROPE_BASE = 1000000.0
EPSILON = 1e-06
NEGATIVE = -1e30
MESH = pl.DeviceIdType.MESH
VMEM_LIMIT = 60 * 1024 * 1024


def rope_tables(positions, width):
    half_width = width // 2
    exponent = jnp.arange(half_width, dtype=jnp.float32) * (2.0 / width)
    inverse = jnp.exp(-exponent * jnp.log(jnp.float32(ROPE_BASE)))
    angles = positions.astype(jnp.float32)[:, None] * inverse[None, :]
    angles = jnp.concatenate([angles, angles], axis=-1)
    return (jnp.cos(angles), jnp.sin(angles))


def remote(src, dst, send_sem, recv_sem, t, c):
    return pltpu.make_async_remote_copy(
        src_ref=src, dst_ref=dst, send_sem=send_sem, recv_sem=recv_sem,
        device_id=(t, c), device_id_type=MESH)


def greet(barrier, t, c, me_t, me_c):
    own = jnp.logical_and(t == me_t, c == me_c)

    @pl.when(jnp.logical_not(own))
    def _():
        pl.semaphore_signal(barrier, inc=1, device_id=(t, c), device_id_type=MESH)

    return own.astype(jnp.int32)


def group_of(c):
    return 8 * ((c // 8 + c % 8) % 8) + c % 8


def holder_of(g):
    return 8 * ((g // 8 - g % 8 + 8) % 8) + g % 8


K0 = 8
V0 = 72
W_CHUNKS = 8


def attention_kernel(x_ref, w_hbm, cos_ref, sin_ref, qg_ref, kg_ref, o_ref,
                     w_buf, acc_ref, heads, blocks, w_sem,
                     s1_send, s1_recv, s2_send, s2_recv, s3_send, s3_recv,
                     s4_send, s4_recv, max_ref, total_ref, sum_ref):
    t = lax.axis_index("tensor")
    c = lax.axis_index("context")
    x, k = t // 2, t % 2
    g = group_of(c)
    chunk = w_buf.shape[1]
    w_copies = [
        pltpu.make_async_copy(w_hbm.at[pl.ds(i * chunk, chunk)], w_buf.at[i], w_sem.at[i])
        for i in range(W_CHUNKS)
    ]
    for w_copy in w_copies:
        w_copy.start()

    head_u = c % QH
    group_u = head_u // 4
    y4 = head_u % 4
    barrier = pltpu.get_barrier_semaphore()
    kept = jnp.int32(0)
    for i in range(8):
        kept += greet(barrier, head_u // 6, holder_of(8 * t + i), t, c)
    for i in range(2):
        kept += greet(barrier, (QH + group_u) // 6, holder_of(8 * t + 2 * y4 + i), t, c)
        kept += greet(barrier, (QH + KVH + group_u) // 6, holder_of(8 * t + 2 * y4 + i), t, c)
    for d in range(1, 4):
        pl.semaphore_signal(barrier, inc=1, device_id=(t, c - y4 + (y4 + d) % 4), device_id_type=MESH)
    for d in range(1, 8):
        pl.semaphore_signal(barrier, inc=1, device_id=((t + d) % 8, c), device_id_type=MESH)

    for i in range(W_CHUNKS):
        w_copies[i].wait()
        at = i % 4 * chunk
        lhs = x_ref[:, i // 4, :, at:at + chunk].reshape(192, chunk)
        part = jnp.dot(lhs, w_buf[i], preferred_element_type=jnp.float32)
        if i == 0:
            acc_ref[...] = part
        else:
            acc_ref[...] += part

    cos_t, sin_t = cos_ref[...], sin_ref[...]
    for j in range(6):
        head = 6 * t + j
        gain = jnp.where(head < QH, qg_ref[...], kg_ref[...])
        for s in range(2):
            raw = acc_ref[96 * s:96 * s + 96, 128 * j:128 * j + 128].astype(jnp.bfloat16)
            wide = raw.astype(jnp.float32)
            mean_sq = jnp.mean(wide * wide, axis=-1, keepdims=True)
            scaled = wide * lax.rsqrt(mean_sq + EPSILON) * gain
            turned = scaled * cos_t + pltpu.roll(scaled, 64, 1) * sin_t
            heads[6 * s + j] = jnp.where(head < QH + KVH, turned, wide).astype(jnp.bfloat16)

    pl.semaphore_wait(barrier, 22 - kept)

    def stage1(b, start):
        s, j = b // 6, b % 6
        head = 6 * t + j
        is_q = head < QH
        i = jnp.maximum(head - QH, 0)
        kind, group = i // KVH, i % KVH
        to_c = s * QH + jnp.where(is_q, head, 4 * group + (g % 8) // 2)
        to_t = g // 8
        slot = jnp.where(is_q, g % 8, K0 + 64 * kind + g)
        sem = jnp.where(is_q, g % 8, 8 + 2 * kind + g % 2)
        own = jnp.logical_and(to_t == t, to_c == c)
        far = remote(heads.at[b], blocks.at[slot], s1_send.at[b], s1_recv.at[sem], to_t, to_c)

        @pl.when(own)
        def _():
            if start:
                pltpu.make_async_copy(heads.at[b], blocks.at[slot], s1_recv.at[sem]).start()

        @pl.when(jnp.logical_not(own))
        def _():
            if start:
                far.start()
            else:
                far.wait_send()

    def land(dst, sem):
        pltpu.make_async_copy(dst, dst, sem).wait()

    for b in range(12):
        stage1(b, True)
    base = 8 * t + 2 * y4
    def stage2(kind, d):
        first = (K0, V0)[kind] + base
        peer = (y4 + d) % 4
        return remote(blocks.at[pl.ds(first, 2)], blocks.at[pl.ds(first, 2)],
                      s2_send.at[kind, d], s2_recv.at[kind, y4], t, c - y4 + peer)

    for kind in range(2):
        for i in range(2):
            land(blocks.at[(K0, V0)[kind] + base + i], s1_recv.at[8 + 2 * kind + i])
        for d in range(1, 4):
            stage2(kind, d).start()

    def slab(kind, tt):
        return blocks.at[pl.ds((K0, V0)[kind] + 8 * tt, 8)]

    def along_x(kind, of, to, n):
        return remote(slab(kind, 2 * of + k), slab(kind, 2 * of + k),
                      s3_send.at[n], s3_recv.at[kind, of], 2 * to + k, c)

    def arrived_x(kind, of):
        land(slab(kind, 2 * of + k), s3_recv.at[kind, of])

    def across(kind, of):
        return remote(slab(kind, 2 * of + k), slab(kind, 2 * of + k),
                      s4_send.at[kind, of], s4_recv.at[kind, of], 2 * x + 1 - k, c)

    def across_here(kind, of):
        last = jnp.where(k == 0, x, x - 1)
        return of <= last

    def hand_on(kind, of):
        @pl.when(across_here(kind, of))
        def _():
            across(kind, of).start()

    own_list = {
        0: [(0, 0, 1), (1, 0, 1), (0, 0, 3), (1, 0, 3)],
        1: [(1, 1, 0), (0, 1, 2), (1, 1, 2)],
        2: [(0, 2, 3), (1, 2, 3)],
        3: [],
    }
    relay_list = {0: [(1, 1, 3)], 1: [(0, 0, 2)], 2: [(0, 1, 3)], 3: [(1, 0, 2)]}
    get_list = {
        0: [],
        1: [(0, 0), (1, 0)],
        2: [(0, 1), (1, 1), (0, 0), (1, 0)],
        3: [(1, 0), (0, 0), (0, 2), (1, 2), (0, 1), (1, 1)],
    }
    for now in range(2):
        for d in range(1, 4):
            peer = (y4 + d) % 4
            land(blocks.at[pl.ds((K0, V0)[now] + 8 * t + 2 * peer, 2)], s2_recv.at[now, peer])
        for xx in range(4):
            @pl.when(x == xx)
            def _(xx=xx):
                for n, (kind, of, to) in enumerate(own_list[xx]):
                    if kind == now:
                        along_x(kind, of, to, n).start()

                @pl.when(k == 0)
                def _():
                    across(now, xx).start()

    score_scale = HD ** (-0.5)
    rows = 384

    def update(state, q, keys, vals, mask):
        old_max, old_total, old_acc = state
        scores = lax.dot_general(q, keys, (((1,), (1,)), ((), ())),
                                 preferred_element_type=jnp.float32) * score_scale
        if mask is not None:
            scores = jnp.where(mask, scores, NEGATIVE)
        new_max = jnp.maximum(old_max, jnp.max(scores, axis=-1, keepdims=True))
        weights = jnp.exp(scores - new_max)
        shrink = jnp.exp(old_max - new_max)
        new_total = old_total * shrink + jnp.sum(weights, axis=-1, keepdims=True)
        new_acc = old_acc * shrink + jnp.dot(
            weights.astype(jnp.bfloat16), vals, preferred_element_type=jnp.float32)
        return new_max, new_total, new_acc

    for i in range(8):
        land(blocks.at[i], s1_recv.at[i])
    for i in range(2):
        q = blocks[0:8].reshape(768, HD)[rows * i:rows * (i + 1)]
        width = rows * (i + 1)
        keys = blocks[pl.ds(K0 + 8 * t, 8)].reshape(768, HD)[:width]
        vals = blocks[pl.ds(V0 + 8 * t, 8)].reshape(768, HD)[:width]
        mask = (lax.broadcasted_iota(jnp.int32, (rows, width), 1)
                <= lax.broadcasted_iota(jnp.int32, (rows, width), 0) + rows * i)
        state = (jnp.full((rows, 1), NEGATIVE, jnp.float32),
                 jnp.zeros((rows, 1), jnp.float32),
                 jnp.zeros((rows, HD), jnp.float32))
        max_ref[i], total_ref[i], sum_ref[i] = update(state, q, keys, vals, mask)

    def attend(i, first, count):
        q = blocks[0:8].reshape(768, HD)[rows * i:rows * (i + 1)]

        def step(of, state):
            keys = blocks[pl.ds(K0 + 8 * (2 * of + first), 8)].reshape(768, HD)
            vals = blocks[pl.ds(V0 + 8 * (2 * of + first), 8)].reshape(768, HD)
            return update(state, q, keys, vals, None)

        return lax.fori_loop(0, count, step, (max_ref[i], total_ref[i], sum_ref[i]))

    for xx in range(4):
        @pl.when(x == xx)
        def _(xx=xx):
            done = set()
            for n, (kind, of, to) in enumerate(relay_list[xx]):
                arrived_x(kind, of)
                done.add((kind, of))
                along_x(kind, of, to, len(own_list[xx]) + n).start()
                if of < xx:
                    across(kind, of).start()
            for kind, of in get_list[xx]:
                if (kind, of) not in done:
                    arrived_x(kind, of)
                    across(kind, of).start()

    for i in range(2):
        max_ref[i], total_ref[i], sum_ref[i] = attend(i, k, x)

    for of in range(4):
        for kind in range(2):
            @pl.when(jnp.where(k == 1, of <= x, of < x))
            def _():
                land(slab(kind, 2 * of + 1 - k), s4_recv.at[kind, of])

    for i in range(2):
        _, total, acc = attend(i, 1 - k, x + k)
        o_ref[0, rows * i:rows * (i + 1), :] = (acc / total).astype(jnp.bfloat16)

    for b in range(12):
        stage1(b, False)
    for kind in range(2):
        for d in range(1, 4):
            stage2(kind, d).wait_send()
    for xx in range(4):
        @pl.when(x == xx)
        def _(xx=xx):
            sends = own_list[xx] + relay_list[xx]
            for n, (kind, of, to) in enumerate(sends):
                along_x(kind, of, to, n).wait_send()
    for of in range(4):
        for kind in range(2):
            @pl.when(across_here(kind, of))
            def _():
                across(kind, of).wait_send()


def attention(normed, w_all, cos_t, sin_t, q_gain, k_gain):
    vmem = pl.BlockSpec(memory_space=pltpu.VMEM)
    dma = pltpu.SemaphoreType.DMA
    return pl.pallas_call(
        attention_kernel,
        out_shape=jax.ShapeDtypeStruct((1, 768, HD), jnp.bfloat16),
        in_specs=[vmem, pl.BlockSpec(memory_space=pl.ANY), vmem, vmem, vmem, vmem],
        out_specs=vmem,
        scratch_shapes=[
            pltpu.VMEM((W_CHUNKS, 4096 // W_CHUNKS, 768), jnp.bfloat16),
            pltpu.VMEM((192, 768), jnp.float32),
            pltpu.VMEM((12, 96, HD), jnp.bfloat16),
            pltpu.VMEM((136, 96, HD), jnp.bfloat16),
            dma((W_CHUNKS,)),
            dma((12,)), dma((12,)),
            dma((2, 4)), dma((2, 4)),
            dma((6,)), dma((2, 4)),
            dma((2, 4)), dma((2, 4)),
            pltpu.VMEM((2, 384, 1), jnp.float32),
            pltpu.VMEM((2, 384, 1), jnp.float32),
            pltpu.VMEM((2, 384, HD), jnp.float32),
        ],
        compiler_params=pltpu.CompilerParams(
            collective_id=1, has_side_effects=True, vmem_limit_bytes=VMEM_LIMIT),
        name="project_exchange_attend",
    )(normed, w_all, cos_t, sin_t, q_gain, k_gain)


VOCAB_PART = 18992
ZERO_ROW = VOCAB_PART


def embed_kernel(ids_ref, table_ref, gain_ref, w_ref, out_ref, w_out,
                 rows_ref, id_row, ids_v, ids_t, ids_s, pairs,
                 for_other, own, from_other, from_x, summed, pieces, wide_ref, normed,
                 ids_send, ids_recv, idx_sem, rs4_send, rs4_recv, rsx_send, rsx_recv,
                 a2a_send, a2a_recv, agx_send, agx_recv, agr_send, agr_recv, agp_send, agp_recv,
                 w_send, w_recv, w_sem):
    t = lax.axis_index("tensor")
    c = lax.axis_index("context")
    z, y = c // 8, c % 8
    keep_w = pltpu.make_async_copy(w_ref, w_out.at[z, y], w_sem)
    keep_w.start()
    x, k = t // 2, t % 2
    other = 2 * x + 1 - k
    barrier = pltpu.get_barrier_semaphore()

    @pl.loop(1, 64)
    def _(i):
        pl.semaphore_signal(barrier, inc=1, device_id=(t, (c + i) % 64), device_id_type=MESH)

    for d in range(1, 8):
        pl.semaphore_signal(barrier, inc=1, device_id=((t + d) % 8, c), device_id_type=MESH)

    twice = (lax.broadcasted_iota(jnp.int32, (64, 128), 1) % 64
             == lax.broadcasted_iota(jnp.int32, (64, 128), 0)).astype(jnp.float32).astype(jnp.bfloat16)

    def transpose(block):
        return lax.dot_general(block, twice, (((0,), (0,)), ((), ())), preferred_element_type=jnp.float32)

    full = VOCAB_PART // 128

    def turn(first, last):
        @pl.loop(first, last, unroll=2)
        def _(b):
            at = pl.multiple_of(b * 128, 128)
            rows_ref[pl.ds(at, 128), :] = transpose(table_ref[:, pl.ds(at, 128)])

    id_row[...] = jnp.zeros_like(id_row)
    id_row[:, :ids_ref.shape[1]] = ids_ref[...]
    turn(0, 50)
    pl.semaphore_wait(barrier, 70)

    def land(dst, sem):
        pltpu.make_async_copy(dst, dst, sem).wait()

    def send_ids(i):
        return remote(id_row, ids_v.at[c], ids_send.at[i], ids_recv.at[c], t, (c + i) % 64)

    @pl.loop(1, 64)
    def _(i):
        send_ids(i).start()

    def w_block(stage, half, at):
        if (stage == 0) == (half == 0):
            return w_out.at[z, at, 0] if half == 0 else w_out.at[pl.ds(0, 8), at, 1]
        return w_out.at[at, pl.ds(0, 8), 0] if half == 0 else w_out.at[at, y, 1]

    def w_step(stage, half, up, step):
        here = y if (stage == 0) == (half == 0) else z
        sign = 1 if up else -1
        block = w_block(stage, half, (here - sign * step) % 8)
        to = (here + sign) % 8
        peer = 8 * z + to if (stage == 0) == (half == 0) else 8 * to + y
        n = step if up else 4 + step
        arriving = w_block(stage, half, (here - sign * (step + 1)) % 8)
        if step == 3:
            size = (16, 4)[stage]
            part = pl.ds(0 if up else size, size)
            block, arriving = block.at[part], arriving.at[part]

        def copy():
            return remote(w_ref.at[half] if (stage, step) == (0, 0) else block, block,
                          w_send.at[stage, half, n], w_recv.at[stage, half, n], t, peer)

        return copy, arriving, w_recv.at[stage, half, n]

    w_rings = [(half, up) for half in range(2) for up in (True, False)]

    def pump(n):
        for step, starting in ((n - 1, False), (n, True)):
            stage, at = step // 4, step % 4
            if not 0 <= stage < 2:
                continue
            for half, up in w_rings:
                copy, arriving, sem = w_step(stage, half, up, at)
                if starting:
                    copy().start()
                else:
                    land(arriving, sem)

    pump(0)
    ids_v[c] = id_row[...]
    turn(50, 84)
    pump(1)
    turn(84, 116)
    pump(2)
    turn(116, full)
    rest = VOCAB_PART - full * 128
    tail = jnp.concatenate(
        [table_ref[:, full * 128:].astype(jnp.float32), jnp.zeros((64, 128 - rest), jnp.float32)], axis=1)
    rows_ref[full * 128:, :] = transpose(tail.astype(jnp.bfloat16))

    pump(3)

    @pl.loop(1, 64)
    def _(i):
        src = (c + i) % 64
        land(ids_v.at[src], ids_recv.at[src])

    for s in range(2):
        local = ids_v[:, s, :] - t * VOCAB_PART
        local = jnp.where(jnp.logical_and(local >= 0, local < VOCAB_PART), local, ZERO_ROW)
        for q in range(4):
            ids_t[4 * s + q] = pltpu.roll(local, 128 - 24 * q, 1) if q else local

    def to_smem(tp):
        return pltpu.make_async_copy(ids_t.at[tp], ids_s.at[tp], idx_sem.at[tp])

    for d in (2, 1, 3, 0):
        for kk in (1 - k, k):
            to_smem(2 * ((x + d) % 4) + kk).start()
    keep_w.wait()
    pump(4)

    first_half = lax.broadcasted_iota(jnp.int32, (16, 128), 1) < 64

    def look_up(tp, dst, n):
        to_smem(tp).wait()

        @pl.loop(0, 32)
        def _(half):
            for m in range(2):
                cc = 2 * half + m
                for i in range(12):
                    first = rows_ref[pl.ds(ids_s[tp, cc, i], 1), :]
                    second = rows_ref[pl.ds(ids_s[tp, cc, 12 + i], 1), :]
                    pairs[m, i:i + 1, :] = jnp.where(first_half[:1], first, second)
            for m in range(2):
                dst[n, 2 * half + m] = pairs[m].astype(jnp.bfloat16)

    pairs[...] = jnp.zeros_like(pairs)

    def to_other(n):
        return remote(for_other.at[n], from_other.at[n], rs4_send.at[n], rs4_recv.at[n], other, c)

    def to_chip(n, xx):
        return remote(own.at[n], from_x.at[n], rsx_send.at[n], rsx_recv.at[n], 2 * xx + k, c)

    for n, d in enumerate((2, 1, 3, 0)):
        xx = (x + d) % 4
        look_up(2 * xx + 1 - k, for_other, n)
        to_other(n).start()
        look_up(2 * xx + k, own, n)
        land(from_other.at[n], rs4_recv.at[n])
        own[n] = own[n] + from_other[n]
        if d:
            to_chip(n, xx).start()

    pump(5)
    for n in range(3):
        land(from_x.at[n], rsx_recv.at[n])
    summed[...] = (own[3] + from_x[0]) + (from_x[1] + from_x[2])

    def send_rows(i):
        peer = (c + i) % 64
        return remote(summed.at[group_of(peer)], pieces.at[c], a2a_send.at[i], a2a_recv.at[c], t, peer)

    @pl.loop(1, 64)
    def _(i):
        send_rows(i).start()

    pieces[c] = summed[group_of(c)]
    pump(6)

    @pl.loop(1, 64)
    def _(i):
        src = (c + i) % 64
        land(pieces.at[src], a2a_recv.at[src])

    pump(7)

    def add_squares(i, acc):
        piece = pieces[i].astype(jnp.float32)
        return acc + piece * piece

    squares = lax.fori_loop(0, 64, add_squares, jnp.zeros((16, 128), jnp.float32))
    sum_low = jnp.sum(jnp.where(first_half, squares, 0.0), axis=-1, keepdims=True)
    sum_high = jnp.sum(jnp.where(first_half, 0.0, squares), axis=-1, keepdims=True)
    scale_low = lax.rsqrt(sum_low / 4096 + EPSILON)
    scale_high = lax.rsqrt(sum_high / 4096 + EPSILON)
    for p in range(32):
        even = pieces[2 * p].astype(jnp.float32)
        odd = pieces[2 * p + 1].astype(jnp.float32)
        gain = gain_ref[:, 128 * p:128 * p + 128]
        low_rows = jnp.where(first_half, even, pltpu.roll(odd, 64, 1)) * scale_low * gain
        high_rows = jnp.where(first_half, pltpu.roll(even, 64, 1), odd) * scale_high * gain
        wide_ref[0:12, 128 * p:128 * p + 128] = low_rows[:12]
        wide_ref[12:24, 128 * p:128 * p + 128] = high_rows[:12]
    for h in range(2):
        part = wide_ref[:, 2048 * h:2048 * h + 2048].astype(jnp.bfloat16)
        normed[h] = part
        out_ref[t, h] = part

    right, left = 2 * ((x + 1) % 4) + k, 2 * ((x + 3) % 4) + k
    across = 2 * ((x + 2) % 4) + k
    to_right = remote(normed, out_ref.at[t], agx_send.at[0], agx_recv.at[0], right, c)
    to_left = remote(normed, out_ref.at[t], agx_send.at[1], agx_recv.at[1], left, c)
    to_right.start()
    to_left.start()

    def hand_over(src, tt, n):
        return remote(src, out_ref.at[tt], agp_send.at[n], agp_recv.at[n], other, c)

    hand_own = hand_over(normed, t, 0)
    hand_own.start()
    land(out_ref.at[left], agx_recv.at[0])
    on_right = remote(out_ref.at[left, 0], out_ref.at[left, 0], agr_send.at[0], agr_recv.at[0], right, c)
    on_right.start()
    hand_left = hand_over(out_ref.at[left], left, 1)
    hand_left.start()
    land(out_ref.at[right], agx_recv.at[1])
    on_left = remote(out_ref.at[right, 1], out_ref.at[right, 1], agr_send.at[1], agr_recv.at[1], left, c)
    on_left.start()
    hand_right = hand_over(out_ref.at[right], right, 2)
    hand_right.start()
    land(out_ref.at[across, 0], agr_recv.at[0])
    land(out_ref.at[across, 1], agr_recv.at[1])
    hand_across = hand_over(out_ref.at[across], across, 3)
    hand_across.start()

    flip = 1 - 2 * k
    land(out_ref.at[t + flip], agp_recv.at[0])
    land(out_ref.at[left + flip], agp_recv.at[1])
    land(out_ref.at[right + flip], agp_recv.at[2])
    land(out_ref.at[across + flip], agp_recv.at[3])

    pump(8)
    for stage in range(2):
        for half, up in w_rings:
            for step in range(4):
                w_step(stage, half, up, step)[0]().wait_send()

    @pl.loop(1, 64)
    def _(i):
        send_ids(i).wait_send()
        send_rows(i).wait_send()

    for n, d in enumerate((2, 1, 3, 0)):
        to_other(n).wait_send()
        if d:
            to_chip(n, (x + d) % 4).wait_send()
    for copy in (to_right, to_left, on_right, on_left, hand_own, hand_left, hand_right, hand_across):
        copy.wait_send()


def embed(ids, table, gain, w_part):
    vmem = pl.BlockSpec(memory_space=pltpu.VMEM)
    dma = pltpu.SemaphoreType.DMA
    slabs = (64, 16, 128)
    return pl.pallas_call(
        embed_kernel,
        out_shape=(jax.ShapeDtypeStruct((8, 2, 24, 2048), jnp.bfloat16),
                   jax.ShapeDtypeStruct((8, 8, 2, 32, 768), jnp.bfloat16)),
        in_specs=[vmem, vmem, vmem, vmem],
        out_specs=(vmem, pl.BlockSpec(memory_space=pl.ANY)),
        scratch_shapes=[
            pltpu.VMEM((VOCAB_PART // 128 * 128 + 128, 128), jnp.float32),
            pltpu.VMEM((2, 128), jnp.int32),
            pltpu.VMEM((64, 2, 128), jnp.int32),
            pltpu.VMEM((8, 64, 128), jnp.int32),
            pltpu.SMEM((8, 64, 128), jnp.int32),
            pltpu.VMEM((2, 16, 128), jnp.float32),
            pltpu.VMEM((4,) + slabs, jnp.bfloat16),
            pltpu.VMEM((4,) + slabs, jnp.bfloat16),
            pltpu.VMEM((4,) + slabs, jnp.bfloat16),
            pltpu.VMEM((3,) + slabs, jnp.bfloat16),
            pltpu.VMEM(slabs, jnp.bfloat16),
            pltpu.VMEM(slabs, jnp.bfloat16),
            pltpu.VMEM((24, 4096), jnp.float32),
            pltpu.VMEM((2, 24, 2048), jnp.bfloat16),
            dma((64,)), dma((64,)), dma((8,)),
            dma((4,)), dma((4,)), dma((3,)), dma((3,)),
            dma((64,)), dma((64,)),
            dma((2,)), dma((2,)), dma((2,)), dma((2,)), dma((4,)), dma((4,)),
            dma((2, 2, 8)), dma((2, 2, 8)), dma,
        ],
        compiler_params=pltpu.CompilerParams(
            collective_id=0, has_side_effects=True, vmem_limit_bytes=VMEM_LIMIT),
        name="look_up_scatter_norm",
    )(ids, table, gain, w_part)


def shards(token_ids, embed_table, input_gain, w_qkv, q_gain, k_gain):
    context_rank = lax.axis_index("context")
    local_len = token_ids.shape[1]
    normed, w_all = embed(token_ids, embed_table, input_gain[None], w_qkv.reshape(2, 32, -1))
    w_all = w_all.reshape(4096, -1)
    positions = group_of(context_rank) * local_len + jnp.arange(local_len, dtype=jnp.int32)
    cos_t, sin_t = rope_tables(positions, HD)
    sin_t = jnp.concatenate([-sin_t[:, :64], sin_t[:, 64:]], axis=-1)
    return attention(normed, w_all, cos_t, sin_t, q_gain[None], k_gain[None])


def solution(mesh):
    return jax.shard_map(
        shards,
        mesh=mesh,
        in_specs=(P(None, "context"), P("context", "tensor"), P(), P("context", "tensor"), P(), P()),
        out_specs=P("context", "tensor", None),
        check_vma=False,
    )
```

```python
import functools

import jax
import jax.numpy as jnp
from jax import lax
from jax.experimental import pallas as pl
from jax.experimental.pallas import tpu as pltpu
from jax.sharding import PartitionSpec as P

QH = 32
KVH = 8
HD = 128
ROPE_BASE = 1000000.0
EPSILON = 1e-06
NEGATIVE = -1e30
MESH = pl.DeviceIdType.MESH
VMEM_LIMIT = 60 * 1024 * 1024


def rope_tables(positions, width):
    half_width = width // 2
    exponent = jnp.arange(half_width, dtype=jnp.float32) * (2.0 / width)
    inverse = jnp.exp(-exponent * jnp.log(jnp.float32(ROPE_BASE)))
    angles = positions.astype(jnp.float32)[:, None] * inverse[None, :]
    angles = jnp.concatenate([angles, angles], axis=-1)
    return (jnp.cos(angles), jnp.sin(angles))


def remote(src, dst, send_sem, recv_sem, t, c):
    return pltpu.make_async_remote_copy(
        src_ref=src, dst_ref=dst, send_sem=send_sem, recv_sem=recv_sem,
        device_id=(t, c), device_id_type=MESH)


def greet(barrier, t, c, me_t, me_c):
    own = jnp.logical_and(t == me_t, c == me_c)

    @pl.when(jnp.logical_not(own))
    def _():
        pl.semaphore_signal(barrier, inc=1, device_id=(t, c), device_id_type=MESH)

    return own.astype(jnp.int32)


def group_of(c):
    return 8 * ((c // 8 + c % 8) % 8) + c % 8


def holder_of(g):
    return 8 * ((g // 8 - g % 8 + 8) % 8) + g % 8


K0 = 8
V0 = 72
W_CHUNKS = 8


def attention_kernel(x_ref, w_hbm, cos_ref, sin_ref, qg_ref, kg_ref, o_ref,
                     w_buf, acc_ref, heads, blocks, w_sem,
                     s1_send, s1_recv, s2_send, s2_recv, s3_send, s3_recv,
                     s4_send, s4_recv, max_ref, total_ref, sum_ref):
    t = lax.axis_index("tensor")
    c = lax.axis_index("context")
    x, k = t // 2, t % 2
    g = group_of(c)
    chunk = w_buf.shape[1]
    w_copies = [
        pltpu.make_async_copy(w_hbm.at[pl.ds(i * chunk, chunk)], w_buf.at[i], w_sem.at[i])
        for i in range(W_CHUNKS)
    ]
    for w_copy in w_copies:
        w_copy.start()

    head_u = c % QH
    group_u = head_u // 4
    y4 = head_u % 4
    barrier = pltpu.get_barrier_semaphore()
    kept = jnp.int32(0)
    for i in range(8):
        kept += greet(barrier, head_u // 6, holder_of(8 * t + i), t, c)
    for i in range(2):
        kept += greet(barrier, (QH + group_u) // 6, holder_of(8 * t + 2 * y4 + i), t, c)
        kept += greet(barrier, (QH + KVH + group_u) // 6, holder_of(8 * t + 2 * y4 + i), t, c)
    for d in range(1, 4):
        pl.semaphore_signal(barrier, inc=1, device_id=(t, c - y4 + (y4 + d) % 4), device_id_type=MESH)
    for d in range(1, 8):
        pl.semaphore_signal(barrier, inc=1, device_id=((t + d) % 8, c), device_id_type=MESH)

    for i in range(W_CHUNKS):
        w_copies[i].wait()
        at = i % 4 * chunk
        lhs = x_ref[:, i // 4, :, at:at + chunk].reshape(192, chunk)
        part = jnp.dot(lhs, w_buf[i], preferred_element_type=jnp.float32)
        if i == 0:
            acc_ref[...] = part
        else:
            acc_ref[...] += part

    cos_t, sin_t = cos_ref[...], sin_ref[...]
    for j in range(6):
        head = 6 * t + j
        gain = jnp.where(head < QH, qg_ref[...], kg_ref[...])
        for s in range(2):
            raw = acc_ref[96 * s:96 * s + 96, 128 * j:128 * j + 128].astype(jnp.bfloat16)
            wide = raw.astype(jnp.float32)
            mean_sq = jnp.mean(wide * wide, axis=-1, keepdims=True)
            scaled = wide * lax.rsqrt(mean_sq + EPSILON) * gain
            turned = scaled * cos_t + pltpu.roll(scaled, 64, 1) * sin_t
            heads[6 * s + j] = jnp.where(head < QH + KVH, turned, wide).astype(jnp.bfloat16)

    pl.semaphore_wait(barrier, 22 - kept)

    def stage1(b, start):
        s, j = b // 6, b % 6
        head = 6 * t + j
        is_q = head < QH
        i = jnp.maximum(head - QH, 0)
        kind, group = i // KVH, i % KVH
        to_c = s * QH + jnp.where(is_q, head, 4 * group + (g % 8) // 2)
        to_t = g // 8
        slot = jnp.where(is_q, g % 8, K0 + 64 * kind + g)
        sem = jnp.where(is_q, g % 8, 8 + 2 * kind + g % 2)
        own = jnp.logical_and(to_t == t, to_c == c)
        far = remote(heads.at[b], blocks.at[slot], s1_send.at[b], s1_recv.at[sem], to_t, to_c)

        @pl.when(own)
        def _():
            if start:
                pltpu.make_async_copy(heads.at[b], blocks.at[slot], s1_recv.at[sem]).start()

        @pl.when(jnp.logical_not(own))
        def _():
            if start:
                far.start()
            else:
                far.wait_send()

    def land(dst, sem):
        pltpu.make_async_copy(dst, dst, sem).wait()

    for b in range(12):
        stage1(b, True)
    base = 8 * t + 2 * y4
    def stage2(kind, d):
        first = (K0, V0)[kind] + base
        peer = (y4 + d) % 4
        return remote(blocks.at[pl.ds(first, 2)], blocks.at[pl.ds(first, 2)],
                      s2_send.at[kind, d], s2_recv.at[kind, y4], t, c - y4 + peer)

    for kind in range(2):
        for i in range(2):
            land(blocks.at[(K0, V0)[kind] + base + i], s1_recv.at[8 + 2 * kind + i])
        for d in range(1, 4):
            stage2(kind, d).start()

    def slab(kind, tt):
        return blocks.at[pl.ds((K0, V0)[kind] + 8 * tt, 8)]

    def along_x(kind, of, to, n):
        return remote(slab(kind, 2 * of + k), slab(kind, 2 * of + k),
                      s3_send.at[n], s3_recv.at[kind, of], 2 * to + k, c)

    def arrived_x(kind, of):
        land(slab(kind, 2 * of + k), s3_recv.at[kind, of])

    def across(kind, of):
        return remote(slab(kind, 2 * of + k), slab(kind, 2 * of + k),
                      s4_send.at[kind, of], s4_recv.at[kind, of], 2 * x + 1 - k, c)

    def across_here(kind, of):
        last = jnp.where(k == 0, x, x - 1)
        return of <= last

    def hand_on(kind, of):
        @pl.when(across_here(kind, of))
        def _():
            across(kind, of).start()

    own_list = {
        0: [(0, 0, 1), (1, 0, 1), (0, 0, 3), (1, 0, 3)],
        1: [(1, 1, 0), (0, 1, 2), (1, 1, 2)],
        2: [(0, 2, 3), (1, 2, 3)],
        3: [],
    }
    relay_list = {0: [(1, 1, 3)], 1: [(0, 0, 2)], 2: [(0, 1, 3)], 3: [(1, 0, 2)]}
    get_list = {
        0: [],
        1: [(0, 0), (1, 0)],
        2: [(0, 1), (1, 1), (0, 0), (1, 0)],
        3: [(1, 0), (0, 0), (0, 2), (1, 2), (0, 1), (1, 1)],
    }
    for now in range(2):
        for d in range(1, 4):
            peer = (y4 + d) % 4
            land(blocks.at[pl.ds((K0, V0)[now] + 8 * t + 2 * peer, 2)], s2_recv.at[now, peer])
        for xx in range(4):
            @pl.when(x == xx)
            def _(xx=xx):
                for n, (kind, of, to) in enumerate(own_list[xx]):
                    if kind == now:
                        along_x(kind, of, to, n).start()

                @pl.when(k == 0)
                def _():
                    across(now, xx).start()

    score_scale = HD ** (-0.5)
    rows = 384

    def update(state, q, keys, vals, mask):
        old_max, old_total, old_acc = state
        scores = lax.dot_general(q, keys, (((1,), (1,)), ((), ())),
                                 preferred_element_type=jnp.float32) * score_scale
        if mask is not None:
            scores = jnp.where(mask, scores, NEGATIVE)
        new_max = jnp.maximum(old_max, jnp.max(scores, axis=-1, keepdims=True))
        weights = jnp.exp(scores - new_max)
        shrink = jnp.exp(old_max - new_max)
        new_total = old_total * shrink + jnp.sum(weights, axis=-1, keepdims=True)
        new_acc = old_acc * shrink + jnp.dot(
            weights.astype(jnp.bfloat16), vals, preferred_element_type=jnp.float32)
        return new_max, new_total, new_acc

    for i in range(8):
        land(blocks.at[i], s1_recv.at[i])
    for i in range(2):
        q = blocks[0:8].reshape(768, HD)[rows * i:rows * (i + 1)]
        width = rows * (i + 1)
        keys = blocks[pl.ds(K0 + 8 * t, 8)].reshape(768, HD)[:width]
        vals = blocks[pl.ds(V0 + 8 * t, 8)].reshape(768, HD)[:width]
        mask = (lax.broadcasted_iota(jnp.int32, (rows, width), 1)
                <= lax.broadcasted_iota(jnp.int32, (rows, width), 0) + rows * i)
        state = (jnp.full((rows, 1), NEGATIVE, jnp.float32),
                 jnp.zeros((rows, 1), jnp.float32),
                 jnp.zeros((rows, HD), jnp.float32))
        max_ref[i], total_ref[i], sum_ref[i] = update(state, q, keys, vals, mask)

    def attend(i, first, count):
        q = blocks[0:8].reshape(768, HD)[rows * i:rows * (i + 1)]

        def step(of, state):
            keys = blocks[pl.ds(K0 + 8 * (2 * of + first), 8)].reshape(768, HD)
            vals = blocks[pl.ds(V0 + 8 * (2 * of + first), 8)].reshape(768, HD)
            return update(state, q, keys, vals, None)

        return lax.fori_loop(0, count, step, (max_ref[i], total_ref[i], sum_ref[i]))

    for xx in range(4):
        @pl.when(x == xx)
        def _(xx=xx):
            done = set()
            for n, (kind, of, to) in enumerate(relay_list[xx]):
                arrived_x(kind, of)
                done.add((kind, of))
                along_x(kind, of, to, len(own_list[xx]) + n).start()
                if of < xx:
                    across(kind, of).start()
            for kind, of in get_list[xx]:
                if (kind, of) not in done:
                    arrived_x(kind, of)
                    across(kind, of).start()

    for i in range(2):
        max_ref[i], total_ref[i], sum_ref[i] = attend(i, k, x)

    for of in range(4):
        for kind in range(2):
            @pl.when(jnp.where(k == 1, of <= x, of < x))
            def _():
                land(slab(kind, 2 * of + 1 - k), s4_recv.at[kind, of])

    for i in range(2):
        _, total, acc = attend(i, 1 - k, x + k)
        o_ref[0, rows * i:rows * (i + 1), :] = (acc / total).astype(jnp.bfloat16)

    for b in range(12):
        stage1(b, False)
    for kind in range(2):
        for d in range(1, 4):
            stage2(kind, d).wait_send()
    for xx in range(4):
        @pl.when(x == xx)
        def _(xx=xx):
            sends = own_list[xx] + relay_list[xx]
            for n, (kind, of, to) in enumerate(sends):
                along_x(kind, of, to, n).wait_send()
    for of in range(4):
        for kind in range(2):
            @pl.when(across_here(kind, of))
            def _():
                across(kind, of).wait_send()


def attention(normed, w_all, cos_t, sin_t, q_gain, k_gain):
    vmem = pl.BlockSpec(memory_space=pltpu.VMEM)
    dma = pltpu.SemaphoreType.DMA
    return pl.pallas_call(
        attention_kernel,
        out_shape=jax.ShapeDtypeStruct((1, 768, HD), jnp.bfloat16),
        in_specs=[vmem, pl.BlockSpec(memory_space=pl.ANY), vmem, vmem, vmem, vmem],
        out_specs=vmem,
        scratch_shapes=[
            pltpu.VMEM((W_CHUNKS, 4096 // W_CHUNKS, 768), jnp.bfloat16),
            pltpu.VMEM((192, 768), jnp.float32),
            pltpu.VMEM((12, 96, HD), jnp.bfloat16),
            pltpu.VMEM((136, 96, HD), jnp.bfloat16),
            dma((W_CHUNKS,)),
            dma((12,)), dma((12,)),
            dma((2, 4)), dma((2, 4)),
            dma((6,)), dma((2, 4)),
            dma((2, 4)), dma((2, 4)),
            pltpu.VMEM((2, 384, 1), jnp.float32),
            pltpu.VMEM((2, 384, 1), jnp.float32),
            pltpu.VMEM((2, 384, HD), jnp.float32),
        ],
        compiler_params=pltpu.CompilerParams(
            collective_id=1, has_side_effects=True, vmem_limit_bytes=VMEM_LIMIT),
        name="project_exchange_attend",
    )(normed, w_all, cos_t, sin_t, q_gain, k_gain)


VOCAB_PART = 18992
ZERO_ROW = VOCAB_PART


def embed_kernel(ids_ref, table_ref, gain_ref, w_ref, out_ref, w_out,
                 rows_ref, id_row, ids_v, ids_t, ids_s, pairs,
                 for_other, own, from_other, from_x, summed, pieces, wide_ref, normed,
                 ids_send, ids_recv, idx_sem, rs4_send, rs4_recv, rsx_send, rsx_recv,
                 a2a_send, a2a_recv, agx_send, agx_recv, agr_send, agr_recv, agp_send, agp_recv,
                 w_send, w_recv, w_sem):
    t = lax.axis_index("tensor")
    c = lax.axis_index("context")
    z, y = c // 8, c % 8
    keep_w = pltpu.make_async_copy(w_ref, w_out.at[z, y], w_sem)
    keep_w.start()
    x, k = t // 2, t % 2
    other = 2 * x + 1 - k
    barrier = pltpu.get_barrier_semaphore()

    @pl.loop(1, 64)
    def _(i):
        pl.semaphore_signal(barrier, inc=1, device_id=(t, (c + i) % 64), device_id_type=MESH)

    for d in range(1, 8):
        pl.semaphore_signal(barrier, inc=1, device_id=((t + d) % 8, c), device_id_type=MESH)

    twice = (lax.broadcasted_iota(jnp.int32, (64, 128), 1) % 64
             == lax.broadcasted_iota(jnp.int32, (64, 128), 0)).astype(jnp.float32).astype(jnp.bfloat16)

    def transpose(block):
        return lax.dot_general(block, twice, (((0,), (0,)), ((), ())), preferred_element_type=jnp.float32)

    full = VOCAB_PART // 128

    def turn(first, last):
        @pl.loop(first, last, unroll=2)
        def _(b):
            at = pl.multiple_of(b * 128, 128)
            rows_ref[pl.ds(at, 128), :] = transpose(table_ref[:, pl.ds(at, 128)])

    id_row[...] = jnp.zeros_like(id_row)
    id_row[:, :ids_ref.shape[1]] = ids_ref[...]
    turn(0, 50)
    pl.semaphore_wait(barrier, 70)

    def land(dst, sem):
        pltpu.make_async_copy(dst, dst, sem).wait()

    def send_ids(i):
        return remote(id_row, ids_v.at[c], ids_send.at[i], ids_recv.at[c], t, (c + i) % 64)

    @pl.loop(1, 64)
    def _(i):
        send_ids(i).start()

    def w_block(stage, half, at):
        if (stage == 0) == (half == 0):
            return w_out.at[z, at, 0] if half == 0 else w_out.at[pl.ds(0, 8), at, 1]
        return w_out.at[at, pl.ds(0, 8), 0] if half == 0 else w_out.at[at, y, 1]

    def w_step(stage, half, up, step):
        here = y if (stage == 0) == (half == 0) else z
        sign = 1 if up else -1
        block = w_block(stage, half, (here - sign * step) % 8)
        to = (here + sign) % 8
        peer = 8 * z + to if (stage == 0) == (half == 0) else 8 * to + y
        n = step if up else 4 + step
        arriving = w_block(stage, half, (here - sign * (step + 1)) % 8)
        if step == 3:
            size = (16, 4)[stage]
            part = pl.ds(0 if up else size, size)
            block, arriving = block.at[part], arriving.at[part]

        def copy():
            return remote(w_ref.at[half] if (stage, step) == (0, 0) else block, block,
                          w_send.at[stage, half, n], w_recv.at[stage, half, n], t, peer)

        return copy, arriving, w_recv.at[stage, half, n]

    w_rings = [(half, up) for half in range(2) for up in (True, False)]

    def pump(n):
        for step, starting in ((n - 1, False), (n, True)):
            stage, at = step // 4, step % 4
            if not 0 <= stage < 2:
                continue
            for half, up in w_rings:
                copy, arriving, sem = w_step(stage, half, up, at)
                if starting:
                    copy().start()
                else:
                    land(arriving, sem)

    pump(0)
    ids_v[c] = id_row[...]
    turn(50, 84)
    pump(1)
    turn(84, 116)
    pump(2)
    turn(116, full)
    rest = VOCAB_PART - full * 128
    tail = jnp.concatenate(
        [table_ref[:, full * 128:].astype(jnp.float32), jnp.zeros((64, 128 - rest), jnp.float32)], axis=1)
    rows_ref[full * 128:, :] = transpose(tail.astype(jnp.bfloat16))

    pump(3)

    @pl.loop(1, 64)
    def _(i):
        src = (c + i) % 64
        land(ids_v.at[src], ids_recv.at[src])

    for s in range(2):
        local = ids_v[:, s, :] - t * VOCAB_PART
        local = jnp.where(jnp.logical_and(local >= 0, local < VOCAB_PART), local, ZERO_ROW)
        for q in range(4):
            ids_t[4 * s + q] = pltpu.roll(local, 128 - 24 * q, 1) if q else local

    def to_smem(tp):
        return pltpu.make_async_copy(ids_t.at[tp], ids_s.at[tp], idx_sem.at[tp])

    for d in (2, 1, 3, 0):
        for kk in (1 - k, k):
            to_smem(2 * ((x + d) % 4) + kk).start()
    keep_w.wait()
    pump(4)

    first_half = lax.broadcasted_iota(jnp.int32, (16, 128), 1) < 64

    def look_up(tp, dst, n):
        to_smem(tp).wait()

        @pl.loop(0, 32)
        def _(half):
            for m in range(2):
                cc = 2 * half + m
                for i in range(12):
                    first = rows_ref[pl.ds(ids_s[tp, cc, i], 1), :]
                    second = rows_ref[pl.ds(ids_s[tp, cc, 12 + i], 1), :]
                    pairs[m, i:i + 1, :] = jnp.where(first_half[:1], first, second)
            for m in range(2):
                dst[n, 2 * half + m] = pairs[m].astype(jnp.bfloat16)

    pairs[...] = jnp.zeros_like(pairs)

    def to_other(n):
        return remote(for_other.at[n], from_other.at[n], rs4_send.at[n], rs4_recv.at[n], other, c)

    def to_chip(n, xx):
        return remote(own.at[n], from_x.at[n], rsx_send.at[n], rsx_recv.at[n], 2 * xx + k, c)

    for n, d in enumerate((2, 1, 3, 0)):
        xx = (x + d) % 4
        look_up(2 * xx + 1 - k, for_other, n)
        to_other(n).start()
        if n == 2:
            pump(5)
        look_up(2 * xx + k, own, n)
        land(from_other.at[n], rs4_recv.at[n])
        own[n] = own[n] + from_other[n]
        if d:
            to_chip(n, xx).start()

    pump(6)
    for n in range(3):
        land(from_x.at[n], rsx_recv.at[n])
    summed[...] = (own[3] + from_x[0]) + (from_x[1] + from_x[2])

    def send_rows(i):
        peer = (c + i) % 64
        return remote(summed.at[group_of(peer)], pieces.at[c], a2a_send.at[i], a2a_recv.at[c], t, peer)

    @pl.loop(1, 64)
    def _(i):
        send_rows(i).start()

    pieces[c] = summed[group_of(c)]
    pump(7)

    @pl.loop(1, 64)
    def _(i):
        src = (c + i) % 64
        land(pieces.at[src], a2a_recv.at[src])

    def add_squares(i, acc):
        piece = pieces[i].astype(jnp.float32)
        return acc + piece * piece

    squares = lax.fori_loop(0, 64, add_squares, jnp.zeros((16, 128), jnp.float32))
    sum_low = jnp.sum(jnp.where(first_half, squares, 0.0), axis=-1, keepdims=True)
    sum_high = jnp.sum(jnp.where(first_half, 0.0, squares), axis=-1, keepdims=True)
    scale_low = lax.rsqrt(sum_low / 4096 + EPSILON)
    scale_high = lax.rsqrt(sum_high / 4096 + EPSILON)
    for p in range(32):
        even = pieces[2 * p].astype(jnp.float32)
        odd = pieces[2 * p + 1].astype(jnp.float32)
        gain = gain_ref[:, 128 * p:128 * p + 128]
        low_rows = jnp.where(first_half, even, pltpu.roll(odd, 64, 1)) * scale_low * gain
        high_rows = jnp.where(first_half, pltpu.roll(even, 64, 1), odd) * scale_high * gain
        wide_ref[0:12, 128 * p:128 * p + 128] = low_rows[:12]
        wide_ref[12:24, 128 * p:128 * p + 128] = high_rows[:12]
    for h in range(2):
        part = wide_ref[:, 2048 * h:2048 * h + 2048].astype(jnp.bfloat16)
        normed[h] = part
        out_ref[t, h] = part

    right, left = 2 * ((x + 1) % 4) + k, 2 * ((x + 3) % 4) + k
    across = 2 * ((x + 2) % 4) + k
    to_right = remote(normed, out_ref.at[t], agx_send.at[0], agx_recv.at[0], right, c)
    to_left = remote(normed, out_ref.at[t], agx_send.at[1], agx_recv.at[1], left, c)
    to_right.start()
    to_left.start()

    def hand_over(src, tt, n):
        return remote(src, out_ref.at[tt], agp_send.at[n], agp_recv.at[n], other, c)

    hand_own = hand_over(normed, t, 0)
    hand_own.start()
    land(out_ref.at[left], agx_recv.at[0])
    on_right = remote(out_ref.at[left, 0], out_ref.at[left, 0], agr_send.at[0], agr_recv.at[0], right, c)
    on_right.start()
    hand_left = hand_over(out_ref.at[left], left, 1)
    hand_left.start()
    land(out_ref.at[right], agx_recv.at[1])
    on_left = remote(out_ref.at[right, 1], out_ref.at[right, 1], agr_send.at[1], agr_recv.at[1], left, c)
    on_left.start()
    hand_right = hand_over(out_ref.at[right], right, 2)
    hand_right.start()
    land(out_ref.at[across, 0], agr_recv.at[0])
    land(out_ref.at[across, 1], agr_recv.at[1])
    hand_across = hand_over(out_ref.at[across], across, 3)
    hand_across.start()

    flip = 1 - 2 * k
    land(out_ref.at[t + flip], agp_recv.at[0])
    land(out_ref.at[left + flip], agp_recv.at[1])
    land(out_ref.at[right + flip], agp_recv.at[2])
    land(out_ref.at[across + flip], agp_recv.at[3])

    pump(8)
    for stage in range(2):
        for half, up in w_rings:
            for step in range(4):
                w_step(stage, half, up, step)[0]().wait_send()

    @pl.loop(1, 64)
    def _(i):
        send_ids(i).wait_send()
        send_rows(i).wait_send()

    for n, d in enumerate((2, 1, 3, 0)):
        to_other(n).wait_send()
        if d:
            to_chip(n, (x + d) % 4).wait_send()
    for copy in (to_right, to_left, on_right, on_left, hand_own, hand_left, hand_right, hand_across):
        copy.wait_send()


def embed(ids, table, gain, w_part):
    vmem = pl.BlockSpec(memory_space=pltpu.VMEM)
    dma = pltpu.SemaphoreType.DMA
    slabs = (64, 16, 128)
    return pl.pallas_call(
        embed_kernel,
        out_shape=(jax.ShapeDtypeStruct((8, 2, 24, 2048), jnp.bfloat16),
                   jax.ShapeDtypeStruct((8, 8, 2, 32, 768), jnp.bfloat16)),
        in_specs=[vmem, vmem, vmem, vmem],
        out_specs=(vmem, pl.BlockSpec(memory_space=pl.ANY)),
        scratch_shapes=[
            pltpu.VMEM((VOCAB_PART // 128 * 128 + 128, 128), jnp.float32),
            pltpu.VMEM((2, 128), jnp.int32),
            pltpu.VMEM((64, 2, 128), jnp.int32),
            pltpu.VMEM((8, 64, 128), jnp.int32),
            pltpu.SMEM((8, 64, 128), jnp.int32),
            pltpu.VMEM((2, 16, 128), jnp.float32),
            pltpu.VMEM((4,) + slabs, jnp.bfloat16),
            pltpu.VMEM((4,) + slabs, jnp.bfloat16),
            pltpu.VMEM((4,) + slabs, jnp.bfloat16),
            pltpu.VMEM((3,) + slabs, jnp.bfloat16),
            pltpu.VMEM(slabs, jnp.bfloat16),
            pltpu.VMEM(slabs, jnp.bfloat16),
            pltpu.VMEM((24, 4096), jnp.float32),
            pltpu.VMEM((2, 24, 2048), jnp.bfloat16),
            dma((64,)), dma((64,)), dma((8,)),
            dma((4,)), dma((4,)), dma((3,)), dma((3,)),
            dma((64,)), dma((64,)),
            dma((2,)), dma((2,)), dma((2,)), dma((2,)), dma((4,)), dma((4,)),
            dma((2, 2, 8)), dma((2, 2, 8)), dma,
        ],
        compiler_params=pltpu.CompilerParams(
            collective_id=0, has_side_effects=True, vmem_limit_bytes=VMEM_LIMIT),
        name="look_up_scatter_norm",
    )(ids, table, gain, w_part)


def shards(token_ids, embed_table, input_gain, w_qkv, q_gain, k_gain):
    context_rank = lax.axis_index("context")
    local_len = token_ids.shape[1]
    normed, w_all = embed(token_ids, embed_table, input_gain[None], w_qkv.reshape(2, 32, -1))
    w_all = w_all.reshape(4096, -1)
    positions = group_of(context_rank) * local_len + jnp.arange(local_len, dtype=jnp.int32)
    cos_t, sin_t = rope_tables(positions, HD)
    sin_t = jnp.concatenate([-sin_t[:, :64], sin_t[:, 64:]], axis=-1)
    return attention(normed, w_all, cos_t, sin_t, q_gain[None], k_gain[None])


def solution(mesh):
    return jax.shard_map(
        shards,
        mesh=mesh,
        in_specs=(P(None, "context"), P("context", "tensor"), P(), P("context", "tensor"), P(), P()),
        out_specs=P("context", "tensor", None),
        check_vma=False,
    )
```
